256 devices in a mesh: fsdp: 64 (over x, y_lo, z), tp: 4 (over y_hi, core).
Axes of the slice: x: 4, y: 4 (y_hi: 2, y_lo: 2; y = y_hi * 2 + y_lo), z: 8, core: 2. Of those that a mesh axis runs over, the one named last changes fastest.
Arguments:
- tokens: bfloat16 [8192, 4096], P('fsdp'), may hold values from -6 to 6
- gate_left: bfloat16 [4096, 1024], P('fsdp', 'tp'), may hold values from -0.09375 to 0.09375
- gate_right: bfloat16 [1024, 14336], P('fsdp', 'tp'), may hold values from -0.1875 to 0.1875
- gate_values: bfloat16 [108, 16384], P('tp', 'fsdp'), may hold values from -0.5 to 0.5
- gate_rows: int32 [108], P('tp'), may hold values from 0 to 31
- gate_cols: int32 [108], P('tp'), may hold values from 0 to 111, as said below
- up_left: bfloat16 [4096, 1024], P('fsdp', 'tp'), may hold values from -0.09375 to 0.09375
- up_right: bfloat16 [1024, 14336], P('fsdp', 'tp'), may hold values from -0.1875 to 0.1875
- up_values: bfloat16 [108, 16384], P('tp', 'fsdp'), may hold values from -0.5 to 0.5
- up_rows: int32 [108], P('tp'), may hold values from 0 to 31
- up_cols: int32 [108], P('tp'), may hold values from 0 to 111, as said below
- grad_hidden: bfloat16 [8192, 14336], P('fsdp', 'tp'), may hold values from -6 to 6
Outputs:
- hidden: bfloat16 [8192, 14336], P('fsdp', 'tp')
- grad_gate_values: float32 [108, 16384], P('tp', 'fsdp')
- grad_up_values: float32 [108, 16384], P('tp', 'fsdp')
The draws below stay inside these ranges and needn't reach their ends.
Inputs may be any that keep to these rules, and one draw needn't show every extreme that they name: `gate_cols`: support blocks of one projection are distinct (row block, column block) pairs; the entries that lie on index t of tp have column blocks from t * 14336 // (128 * 4) to (t + 1) * 14336 // (128 * 4) - 1. Rows and columns of one projection go together. `up_cols`: as for the gate projection.
All inputs are finite; a program needn't handle non-finite values.
Results may differ from the reference program's by a relative error of at most 0.005.
Values may be sent and summed in bfloat16 or wider, within the bound.
A program may use at most 128 MiB of HBM per device.

```python
import jax
import jax.numpy as jnp
from jax import lax

D = 4096
FF = 14336
R = 1024
BLK = 128
BLK_TP = 27
TOKENS = 8192
NBLK = 108
N_TP = 4


def support_cells(key):
    row_blocks = D // BLK
    col_blocks = FF // BLK // N_TP

    def one(device):
        shuffled = jax.random.permutation(jax.random.fold_in(key, device), row_blocks * col_blocks)[:BLK_TP]
        return (shuffled // col_blocks, device * col_blocks + shuffled % col_blocks)
    rows, cols = jax.vmap(one)(jnp.arange(N_TP))
    return (rows.reshape(-1).astype(jnp.int32), cols.reshape(-1).astype(jnp.int32))


def draw_gate_rows(key, part):
    return support_cells(jax.random.fold_in(key, 11))[0]


def draw_gate_cols(key, part):
    return support_cells(jax.random.fold_in(key, 11))[1]


def draw_up_rows(key, part):
    return support_cells(jax.random.fold_in(key, 12))[0]


def draw_up_cols(key, part):
    return support_cells(jax.random.fold_in(key, 12))[1]


def levels(key, shape, shards, least, high):
    level = 1.0
    for dim, blocks in shards:
        heights = jax.random.uniform(jax.random.fold_in(jax.random.fold_in(key, 6), dim), (blocks,), jnp.float32, least / len(shards), high / len(shards))
        level = level * jnp.repeat(jnp.exp(heights), shape[dim] // blocks).reshape((-1,) + (1,) * (len(shape) - 1 - dim))
    return level


def bell_draw(rng, extent, spread, reach, cuts=(), dtype=jnp.bfloat16):
    values = jax.random.normal(rng, extent, jnp.float32) * spread
    if len(cuts) > 0:
        values = levels(rng, extent, cuts, -0.22, 0.18) * values
    return jnp.clip(values, min=-reach, max=reach).astype(dtype)


def setup_inputs(seed: int = 0) -> dict:
    splits = jax.random.split(jax.random.key(seed), 13)
    tokens = bell_draw(splits[0], (TOKENS, D), 1.0, 6.0, ((0, 64),))
    gate_left = bell_draw(splits[1], (D, R), D ** -0.5, 0.09375, ((0, 64), (1, 4)))
    gate_right = bell_draw(splits[2], (R, FF), R ** -0.5, 0.1875, ((0, 64), (1, 4)))
    gate_values = bell_draw(splits[3], (NBLK, BLK * BLK), BLK ** -0.5, 0.5, ((0, 4), (1, 64)))
    gate_rows = draw_gate_rows(jax.random.fold_in(splits[12], 71), 0)
    gate_cols = draw_gate_cols(jax.random.fold_in(splits[12], 71), 0)
    up_left = bell_draw(splits[6], (D, R), D ** -0.5, 0.09375, ((0, 64), (1, 4)))
    up_right = bell_draw(splits[7], (R, FF), R ** -0.5, 0.1875, ((0, 64), (1, 4)))
    up_values = bell_draw(splits[8], (NBLK, BLK * BLK), BLK ** -0.5, 0.5, ((0, 4), (1, 64)))
    up_rows = draw_up_rows(jax.random.fold_in(splits[12], 71), 0)
    up_cols = draw_up_cols(jax.random.fold_in(splits[12], 71), 0)
    grad_hidden = bell_draw(splits[11], (TOKENS, FF), 1.0, 6.0, ((0, 64), (1, 4)))
    return dict(tokens=tokens, gate_left=gate_left, gate_right=gate_right, gate_values=gate_values, gate_rows=gate_rows, gate_cols=gate_cols, up_left=up_left, up_right=up_right, up_values=up_values, up_rows=up_rows, up_cols=up_cols, grad_hidden=grad_hidden)


def add_support(source_all, values, rows, cols, total):
    def step(index, acc):
        block = values[index].reshape(BLK, BLK)
        source = lax.dynamic_slice_in_dim(source_all, rows[index] * BLK, BLK, 1)
        start = cols[index] * BLK
        current = lax.dynamic_slice_in_dim(acc, start, BLK, 1)
        update = current + jnp.dot(source, block, preferred_element_type=jnp.float32)
        return lax.dynamic_update_slice_in_dim(acc, update, start, 1)
    return lax.fori_loop(0, values.shape[0], step, total)


def value_grads(tokens, grad_all, rows, cols):
    def one(index):
        left = lax.dynamic_slice_in_dim(tokens, rows[index] * BLK, BLK, 1)
        right = lax.dynamic_slice_in_dim(grad_all, cols[index] * BLK, BLK, 1)
        return jnp.dot(left.T, right, preferred_element_type=jnp.float32).reshape(BLK * BLK)
    return lax.map(one, jnp.arange(rows.shape[0]))


def reference(tokens, gate_left, gate_right, gate_values, gate_rows, gate_cols, up_left, up_right, up_values, up_rows, up_cols, grad_hidden):
    rank_gate = jnp.dot(tokens, gate_left, preferred_element_type=jnp.float32).astype(jnp.bfloat16)
    rank_up = jnp.dot(tokens, up_left, preferred_element_type=jnp.float32).astype(jnp.bfloat16)
    pre_gate = jnp.dot(rank_gate, gate_right, preferred_element_type=jnp.float32)
    pre_gate = add_support(tokens, gate_values, gate_rows, gate_cols, pre_gate)
    pre_up = jnp.dot(rank_up, up_right, preferred_element_type=jnp.float32)
    pre_up = add_support(tokens, up_values, up_rows, up_cols, pre_up)
    sigma = jax.nn.sigmoid(pre_gate)
    silu = pre_gate * sigma
    hidden = (silu * pre_up).astype(jnp.bfloat16)
    upstream = grad_hidden.astype(jnp.float32)
    dpre_gate = (upstream * pre_up * sigma * (1.0 + pre_gate * (1.0 - sigma))).astype(jnp.bfloat16)
    dpre_up = (upstream * silu).astype(jnp.bfloat16)
    grad_gate_values = value_grads(tokens, dpre_gate, gate_rows, gate_cols)
    grad_up_values = value_grads(tokens, dpre_up, up_rows, up_cols)
    return hidden, grad_gate_values, grad_up_values
```

```python
import heapq

import jax
import jax.numpy as jnp
from jax import lax
from jax.experimental import pallas as pl
from jax.experimental.pallas import tpu as pltpu
from jax.sharding import Mesh
from jax.sharding import PartitionSpec as P

BLK = 128
NX, NL, NZ, NH, NC = 4, 2, 8, 2, 2
FSDP = ("x", "yl", "z")
TP = ("yh", "c")
KB = 27
HALF = 1792
TILE = 256
PART_A = 768
ALL = slice(None)
F32, BF16 = jnp.float32, jnp.bfloat16


def dot(a, b):
    return jnp.dot(a, b, preferred_element_type=F32)


class Net:
    LATENCY = 1.5
    RATE = {"x+": 0.045, "x-": 0.045, "z+": 0.045, "z-": 0.045, "y": 0.045, "c": 0.2}

    def __init__(self, send_sems, recv_sems):
        self.sems = (send_sems, recv_sems)
        self.now, self.free, self.heap, self.copies, self.spare = 0.0, {}, [], [], []

    def copy(self, src, dst, where):
        i = len(self.copies)
        made = pltpu.make_async_remote_copy(
            src_ref=src,
            dst_ref=dst,
            send_sem=self.sems[0].at[i],
            recv_sem=self.sems[1].at[i],
            device_id=where,
            device_id_type=pl.DeviceIdType.MESH,
        )
        return made

    def track(self, made, link, size, then):
        self.copies.append(made)
        begin = max(self.now, self.free.get(link, 0.0))
        self.free[link] = begin + size / self.RATE[link]
        heapq.heappush(self.heap, (self.free[link] + self.LATENCY, len(self.copies), made, then))

    def send(self, src, dst, where, link, size, then):
        made = self.copy(src, dst, where)
        made.start()
        self.track(made, link, size, then)

    def work(self, cost, do):
        do()
        self.now += cost

    def run(self):
        while self.heap:
            at, _, made, then = heapq.heappop(self.heap)
            while self.spare and self.now + self.spare[0][0] <= at + 0.5:
                self.work(*self.spare.pop(0))
            self.now = max(self.now, at)
            made.wait_recv()
            then()
        while self.spare:
            self.work(*self.spare.pop(0))

    def finish(self):
        for made in self.copies:
            made.wait_send()


class Count:
    def __init__(self, n, then):
        self.n, self.then = n, then

    def __call__(self):
        self.n -= 1
        if self.n == 0:
            self.then()


def ring_gather(net, n, me, axis, block, size, done):
    reach = n // 2
    left_over = Count(2 * reach, done)

    def step(way, s):
        whose = lax.rem(me - way * (s - 1) + n, n)
        half = ALL if s < reach else (0 if way == 1 else 1)
        ref = block(whose, half)
        to = lax.rem(me + way + n, n)
        net.send(
            ref,
            ref,
            {axis: to},
            axis + ("+" if way == 1 else "-"),
            size if s < reach else size / 2,
            lambda: arrived(way, s),
        )

    def arrived(way, s):
        if s < reach:
            step(way, s + 1)
        left_over()

    step(1, 1)
    step(-1, 1)


def kernel(
    tok,
    gate_left,
    gate_right,
    gate_values,
    gate_rows,
    gate_cols,
    up_left,
    up_right,
    up_values,
    up_rows,
    up_cols,
    grad_hidden,
    table,
    hidden,
    out_gate,
    out_up,
    t_all,
    t_perm,
    t_turn,
    left,
    right,
    shards,
    blocks,
    rank,
    pre,
    chain,
    up_stream,
    dpre,
    back,
    grads,
    came_up,
    came_down,
    mine,
    parcels,
    arrived_parcels,
    send_sems,
    recv_sems,
    local_sems,
):
    x, yl, z = lax.axis_index("x"), lax.axis_index("yl"), lax.axis_index("z")
    yh, c = lax.axis_index("yh"), lax.axis_index("c")
    other = 1 - yl

    def round_x(d):
        return lax.rem(x + d + NX, NX)

    def round_z(d):
        return lax.rem(z + d + NZ, NZ)

    pair, twin = {"yl": other}, {"c": 1 - c}
    across, beyond = {"yh": 1 - yh}, {"yh": 1 - yh, "yl": other}
    near = [{"x": round_x(d), "yl": yl if e == 0 else other} for d in range(NX) for e in range(NL)][1:]
    greeted = [twin, across, beyond, {"z": round_z(1)}, {"z": round_z(-1)}, *near]
    barrier = pltpu.get_barrier_semaphore()
    for who in greeted:
        pl.semaphore_signal(barrier, inc=1, device_id=who, device_id_type=pl.DeviceIdType.MESH)

    keeps = []

    def keep(src, dst):
        made = pltpu.make_async_copy(src, dst, local_sems.at[len(keeps)])
        made.start()
        keeps.append(made)

    def cols(ref, which):
        return ref.at[:, pl.ds(pl.multiple_of(which * HALF, BLK), HALF)]

    own_rows = pl.ds(pl.multiple_of(yl * BLK, BLK), BLK)
    other_rows = pl.ds(pl.multiple_of(other * BLK, BLK), BLK)
    keep(cols(gate_right, yl), right.at[x, yl, z, :, 0:HALF])
    keep(cols(up_right, yl), right.at[x, yl, z, :, HALF : 2 * HALF])
    keep(tok, t_all.at[own_rows])
    keep(cols(grad_hidden, yl), up_stream.at[own_rows])
    own_left = pltpu.make_async_copy(gate_left, left.at[x, yl, z], local_sems.at[len(keeps)])

    @pl.when(yl == 0)
    def _():
        own_left.start()

    @pl.when(yl == 1)
    def _():
        pltpu.make_async_copy(up_left, left.at[x, yl, z], local_sems.at[len(keeps)]).start()

    keeps.append(own_left)
    shards[x, yl] = jnp.zeros((2, 32, 2 * BLK), BF16)
    shards[x, yl, 0, 0:KB] = gate_values[...]
    shards[x, yl, 1, 0:KB] = up_values[...]

    pl.semaphore_wait(barrier, len(greeted))
    net = Net(send_sems, recv_sems)

    def do_rank():
        total = jnp.zeros((2 * BLK, TILE), F32)
        for i in range(NX):
            total += dot(t_all[:, i * 1024 : (i + 1) * 1024], left[i].reshape(1024, TILE))
        slot = yl * 4 + yh * 2 + c
        rank[slot] = total.astype(BF16)

    def rank_slot(l, h, core):
        return rank.at[l * 4 + h * 2 + core]

    def share_rank():
        def on(l, h):
            ref = rank_slot(l, h, c)
            net.send(ref, ref, twin, "c", 0.131, rank_there)

        ref = rank_slot(yl, yh, c)
        net.send(ref, ref, pair, "y", 0.131, lambda: on(other, yh))
        net.send(ref, ref, beyond, "y", 0.0, lambda: on(other, 1 - yh))
        net.send(ref, ref, across, "y", 0.0, lambda: on(yl, 1 - yh))
        on(yl, yh)

    def low_rank(first, last):
        def do(j, _):
            g = (j >= 7).astype(jnp.int32)
            at = pl.ds(pl.multiple_of(j * TILE, TILE), TILE)
            total = jnp.zeros((2 * BLK, TILE), F32)
            for i in range(NX):
                total += dot(rank[g * 4 + i], right[i, :, :, :, at].reshape(TILE, TILE))
            pre[j] = total
            return 0

        lax.fori_loop(first, last, do, 0)

    tiles_a, tiles = PART_A // TILE, 2 * HALF // TILE
    product_a = Count(2, lambda: net.work(1.5, lambda: low_rank(0, tiles_a)))
    product_b = Count(2, lambda: net.work(5.0, lambda: low_rank(tiles_a, tiles)))

    def all_ranks():
        product_a()
        product_b()

    rank_there = Count(7 - 3, all_ranks)

    def rank_ready():
        net.work(2.5, do_rank)
        share_rank()

    left_parts = Count(2 + 1, rank_ready)

    def permute_tokens(first, last):
        def do(r, _):
            part = t_all[:, pl.ds(pl.multiple_of(r * BLK, BLK), BLK)]
            new = lax.broadcasted_iota(jnp.int32, (BLK, BLK), 0)
            old = lax.broadcasted_iota(jnp.int32, (BLK, BLK), 1)

            def source(m):
                shard = ((m >> 1) & 3) * 16 + (m & 1) * 8 + (m >> 4)
                return shard * 2 + ((m >> 3) & 1)

            turn = (source(new) == old).astype(F32).astype(BF16)
            straight = (source(old) == new).astype(F32).astype(BF16)
            t_perm[r] = dot(part, straight).astype(BF16)
            t_turn[r] = lax.dot_general(
                turn, part, (((1,), (1,)), ((), ())), preferred_element_type=F32
            ).astype(BF16)
            return 0

        lax.fori_loop(first, last, do, 0)

    def sparse(g, rows_ref, first, last):
        def do(k, _):
            piece = dot(t_perm[rows_ref[k]], blocks[g * KB + k])
            chain[g * 28 + k + 1] = piece + chain[g * 28 + table[g * 64 + k]]
            return 0

        lax.fori_loop(first, last, do, 0)

    def zero_chain():
        chain[0] = jnp.zeros((2 * BLK, BLK), F32)
        chain[28] = jnp.zeros((2 * BLK, BLK), F32)

    def all_sparse():
        net.spare.append((0.2, zero_chain))
        for g, rows_ref in ((0, gate_rows), (1, up_rows)):
            for first in range(0, KB, 9):
                net.spare.append((2.0, lambda a=(g, rows_ref, first, first + 9): sparse(*a)))

    sparse_ready = Count(2, all_sparse)

    def tokens_there():
        left_parts()
        for first in range(0, 32, 8):
            net.spare.append((1.2, lambda a=(first, first + 8): permute_tokens(*a)))
        sparse_ready()

    def spread_values():
        row = lax.broadcasted_iota(jnp.int32, (KB * 16, 512), 0)
        col = lax.broadcasted_iota(jnp.int32, (KB * 16, 512), 1)
        pick = col == (((row >> 3) & 1) * 256 + (row & 7) * 32 + (row >> 4))
        pick = pick.astype(F32).astype(BF16)
        for g in range(2):
            flat = shards[:, :, g].reshape(256, 2 * BLK)
            tall = jnp.concatenate([flat[:, :BLK], flat[:, BLK:]], axis=0)
            laid = dot(pick, tall).astype(BF16).reshape(KB, 16, BLK)
            blocks[g * KB : (g + 1) * KB, pl.ds(pl.multiple_of(z * 16, 16), 16), :] = laid

    def value_slice(i, half):
        some = {0: slice(0, KB), 1: slice(KB, 2 * KB)}.get(half if isinstance(half, int) else None, ALL)
        return blocks.at[some, pl.ds(pl.multiple_of(i * 16, 16), 16), :]

    def values_near():
        net.work(1.5, spread_values)
        ring_gather(net, NZ, z, "z", value_slice, 0.221, sparse_ready)

    def gather_left():
        a, b = slice(0, 32), slice(32, 64)

        def a_far():
            ring_gather(net, NZ, z, "z", lambda i, h: left.at[:, h, i, a], 0.131, left_parts)

        def b_far():
            ring_gather(net, NX, x, "x", lambda i, h: left.at[i, h, :, b], 0.262, left_parts)

        ring_gather(net, NX, x, "x", lambda i, h: left.at[i, h, z, a], 0.033, a_far)
        ring_gather(net, NZ, z, "z", lambda i, h: left.at[x, h, i, b], 0.033, b_far)

    def gather_right():
        a, b = slice(0, PART_A), slice(PART_A, 2 * HALF)
        size_a, size_b = PART_A * 64e-6, (2 * HALF - PART_A) * 64e-6

        def a_far():
            ring_gather(net, NZ, z, "z", lambda i, h: right.at[:, h, i, :, a], 4 * size_a, product_a)

        def b_far():
            ring_gather(net, NX, x, "x", lambda i, h: right.at[i, h, :, :, b], 8 * size_b, product_b)

        ring_gather(net, NX, x, "x", lambda i, h: right.at[i, h, z, :, a], size_a, a_far)
        ring_gather(net, NZ, z, "z", lambda i, h: right.at[x, h, i, :, b], size_b, b_far)

    swap_left = net.copy(up_left, left.at[x, yl, z], pair)

    @pl.when(yl == 0)
    def _():
        swap_left.start()

    @pl.when(yl == 1)
    def _():
        net.copy(gate_left, left.at[x, yl, z], pair).start()

    for made in keeps:
        made.wait()
    net.track(swap_left, "y", 0.033, gather_left)
    swapped_right = Count(2, gather_right)
    net.send(cols(gate_right, other), right.at[x, yl, z, :, 0:HALF], pair, "y", 0.057, swapped_right)
    net.send(
        cols(up_right, other), right.at[x, yl, z, :, HALF : 2 * HALF], pair, "y", 0.057, swapped_right
    )
    net.send(
        shards.at[x, yl],
        shards.at[x, yl],
        pair,
        "y",
        0.033,
        lambda: ring_gather(net, NX, x, "x", lambda i, h: shards.at[i, h], 0.066, values_near),
    )
    mine_half = pl.ds(pl.multiple_of(c * 64, 64), 64)
    sent_half = pl.ds(pl.multiple_of(yl * BLK + c * 64, 64), 64)
    got_half = pl.ds(pl.multiple_of(other * BLK + c * 64, 64), 64)
    net.send(
        tok.at[mine_half],
        t_all.at[sent_half],
        pair,
        "y",
        0.524,
        lambda: net.send(t_all.at[got_half], t_all.at[got_half], twin, "c", 0.524, tokens_there),
    )
    net.send(cols(grad_hidden, other), up_stream.at[own_rows], pair, "y", 0.459, lambda: None)
    net.run()

    def gated(j, _):
        for h in range(2):
            for rows, mine_too in ((other_rows, False), (own_rows, True)):
                lanes = slice(h * BLK, (h + 1) * BLK)
                col = j * 2 + h
                gate = pre[j, rows, lanes] + chain[table[32 + yl * 14 + col], rows, :]
                up = pre[7 + j, rows, lanes] + chain[28 + table[96 + yl * 14 + col], rows, :]
                coming = up_stream[rows, pl.ds(pl.multiple_of(col * BLK, BLK), BLK)].astype(F32)
                sigma = jax.nn.sigmoid(gate)
                silu = gate * sigma
                unit = (silu * up).astype(BF16)
                dpre[col, rows, :] = (coming * up * sigma * (1.0 + gate * (1.0 - sigma))).astype(BF16)
                dpre[14 + col, rows, :] = (coming * silu).astype(BF16)
                if mine_too:
                    hidden[:, pl.ds(pl.multiple_of(yl * HALF + col * BLK, BLK), BLK)] = unit
                else:
                    back[:, pl.ds(pl.multiple_of(col * BLK, BLK), BLK)] = unit
        return 0

    lax.fori_loop(0, 7, gated, 0)
    net.send(back, cols(hidden, yl), pair, "y", 0.459, lambda: None)

    for g, rows_ref, cols_ref in ((0, gate_rows, gate_cols), (1, up_rows, up_cols)):

        def gradient(k, _, g=g, rows_ref=rows_ref, cols_ref=cols_ref):
            col = cols_ref[k] - (yh * 2 + c) * 28 - yl * 14
            inside = (col >= 0) & (col < 14)
            term = dot(t_turn[rows_ref[k]], dpre[g * 14 + jnp.clip(col, 0, 13)])
            grads[g * KB + k] = jnp.where(inside, term, 0.0)
            return 0

        lax.fori_loop(0, KB, gradient, 0)

    def lot(i, part=16, skip=0):
        return pl.ds(pl.multiple_of(i * 16 + skip, 8), part)

    def exchange():
        mine[...] = (grads[:, lot(z), :] + came_up[3] + came_down[3]).reshape(2 * KB * 16, BLK)
        for s in range(8):
            for g in range(2):
                for p in range(2):
                    rows = pl.ds(g * KB * 16 + p * 8 + s, KB, stride=16)
                    parcels[s, g * 32 : g * 32 + KB, p * BLK : (p + 1) * BLK] = mine[rows, :]
        for d in range(NX):
            for e in range(NL):
                if d == 0 and e == 0:
                    continue
                to_x, to_l = round_x(d), (yl if e == 0 else other)
                net.send(
                    parcels.at[to_x * 2 + to_l],
                    arrived_parcels.at[d * 2 + e],
                    {"x": to_x, "yl": to_l},
                    "x+",
                    0.065,
                    lambda: None,
                )

    home = Count(2, exchange)

    def pass_on(way, j):
        buf = came_up if way == 1 else came_down
        whose = round_z(way * (5 - j))
        if j == 1:
            skip = 0 if way == 1 else 8
            src = grads.at[:, lot(whose, 8, skip), :]
            dst = buf.at[0, :, 0:8]
        else:
            src, dst = grads.at[:, lot(whose), :], buf.at[j - 1]
        net.send(
            src,
            dst,
            {"z": round_z(way)},
            "z+" if way == 1 else "z-",
            0.221 if j == 1 else 0.442,
            lambda: summed(way, j),
        )

    def summed(way, j):
        buf = came_up if way == 1 else came_down
        if j == 4:
            home()
            return
        whose = round_z(way * (4 - j))
        if j == 1:
            at = lot(whose, 8, 0 if way == 1 else 8)
            grads[:, at, :] = grads[:, at, :] + buf[0, :, 0:8, :]
        else:
            at = lot(whose)
            grads[:, at, :] = grads[:, at, :] + buf[j - 1]
        pass_on(way, j + 1)

    pass_on(1, 1)
    pass_on(-1, 1)
    net.run()
    total = parcels[x * 2 + yl]
    for i in range(1, 8):
        total = total + arrived_parcels[i]
    out_gate[...] = total[0:KB]
    out_up[...] = total[32 : 32 + KB]
    net.finish()


def chains(gate_cols, up_cols, base):
    cols = jnp.stack([gate_cols, up_cols]) - base
    index = jnp.arange(64, dtype=jnp.int32)
    padded = jnp.pad(cols, ((0, 0), (0, 64 - KB)))
    asked = jnp.where(index < 32, padded, index - 32)
    limit = jnp.where(index < 32, index, KB)
    earlier = jnp.arange(KB, dtype=jnp.int32)
    hit = (cols[:, None, :] == asked[:, :, None]) & (earlier < limit[:, None])
    return jnp.max(jnp.where(hit, earlier + 1, 0), axis=2).reshape(128)


def on_device(*args):
    base = (lax.axis_index("yh") * 2 + lax.axis_index("c")) * 28
    table = chains(args[5], args[10], base)
    vmem, smem = pl.BlockSpec(memory_space=pltpu.VMEM), pl.BlockSpec(memory_space=pltpu.SMEM)
    specs = [vmem, vmem, vmem, vmem, smem, smem, vmem, vmem, vmem, smem, smem, vmem, smem]
    copies = 110
    return pl.pallas_call(
        kernel,
        out_shape=(
            jax.ShapeDtypeStruct((BLK, 2 * HALF), BF16),
            jax.ShapeDtypeStruct((KB, 2 * BLK), F32),
            jax.ShapeDtypeStruct((KB, 2 * BLK), F32),
        ),
        in_specs=specs,
        out_specs=(vmem, vmem, vmem),
        scratch_shapes=[
            pltpu.VMEM((2 * BLK, 4096), BF16),
            pltpu.VMEM((32, 2 * BLK, BLK), BF16),
            pltpu.VMEM((32, BLK, 2 * BLK), BF16),
            pltpu.VMEM((NX, NL, NZ, 64, TILE), BF16),
            pltpu.VMEM((NX, NL, NZ, 16, 2 * HALF), BF16),
            pltpu.VMEM((NX, NL, 2, 32, 2 * BLK), BF16),
            pltpu.VMEM((2 * KB, BLK, BLK), BF16),
            pltpu.VMEM((8, 2 * BLK, TILE), BF16),
            pltpu.VMEM((14, 2 * BLK, TILE), F32),
            pltpu.VMEM((56, 2 * BLK, BLK), F32),
            pltpu.VMEM((2 * BLK, HALF), BF16),
            pltpu.VMEM((28, 2 * BLK, BLK), BF16),
            pltpu.VMEM((BLK, HALF), BF16),
            pltpu.VMEM((2 * KB, BLK, BLK), F32),
            pltpu.VMEM((4, 2 * KB, 16, BLK), F32),
            pltpu.VMEM((4, 2 * KB, 16, BLK), F32),
            pltpu.VMEM((2 * KB * 16, BLK), F32),
            pltpu.VMEM((8, 64, 2 * BLK), F32),
            pltpu.VMEM((8, 64, 2 * BLK), F32),
            pltpu.SemaphoreType.DMA((copies,)),
            pltpu.SemaphoreType.DMA((copies,)),
            pltpu.SemaphoreType.DMA((8,)),
        ],
        compiler_params=pltpu.CompilerParams(
            collective_id=0, has_side_effects=True, vmem_limit_bytes=58 * 2**20
        ),
    )(*args, table)


def solution(mesh):
    finer = Mesh(mesh.devices.reshape(NX, NL, NZ, NH, NC), (*FSDP, *TP))
    return jax.shard_map(
        on_device,
        mesh=finer,
        in_specs=(
            P(FSDP, None),
            P(FSDP, TP),
            P(FSDP, TP),
            P(TP, FSDP),
            P(TP),
            P(TP),
            P(FSDP, TP),
            P(FSDP, TP),
            P(TP, FSDP),
            P(TP),
            P(TP),
            P(FSDP, TP),
        ),
        out_specs=(P(FSDP, TP), P(TP, FSDP), P(TP, FSDP)),
        check_vma=False,
    )
```

```python
import heapq

import jax
import jax.numpy as jnp
from jax import lax
from jax.experimental import pallas as pl
from jax.experimental.pallas import tpu as pltpu
from jax.sharding import Mesh
from jax.sharding import PartitionSpec as P

BLK = 128
NX, NL, NZ, NH, NC = 4, 2, 8, 2, 2
FSDP = ("x", "yl", "z")
TP = ("yh", "c")
KB = 27
HALF = 1792
TILE = 256
PART_A = 768
ALL = slice(None)
F32, BF16 = jnp.float32, jnp.bfloat16


def dot(a, b):
    return jnp.dot(a, b, preferred_element_type=F32)


class Net:
    LATENCY = 3.0
    RATE = {"x+": 0.045, "x-": 0.045, "z+": 0.045, "z-": 0.045, "y": 0.045, "c": 0.2}

    def __init__(self, send_sems, recv_sems):
        self.sems = (send_sems, recv_sems)
        self.now, self.free, self.heap, self.copies, self.spare = 0.0, {}, [], [], []

    def copy(self, src, dst, where):
        i = len(self.copies)
        made = pltpu.make_async_remote_copy(
            src_ref=src,
            dst_ref=dst,
            send_sem=self.sems[0].at[i],
            recv_sem=self.sems[1].at[i],
            device_id=where,
            device_id_type=pl.DeviceIdType.MESH,
        )
        return made

    def track(self, made, link, size, then):
        self.copies.append(made)
        begin = max(self.now, self.free.get(link, 0.0))
        self.free[link] = begin + size / self.RATE[link]
        heapq.heappush(self.heap, (self.free[link] + self.LATENCY, len(self.copies), made, then))

    def send(self, src, dst, where, link, size, then):
        made = self.copy(src, dst, where)
        made.start()
        self.track(made, link, size, then)

    def work(self, cost, do):
        do()
        self.now += cost

    def run(self):
        while self.heap:
            at, _, made, then = heapq.heappop(self.heap)
            while self.spare and self.now + self.spare[0][0] <= at + 0.5:
                self.work(*self.spare.pop(0))
            self.now = max(self.now, at)
            made.wait_recv()
            then()
        while self.spare:
            self.work(*self.spare.pop(0))

    def finish(self):
        for made in self.copies:
            made.wait_send()


class Count:
    def __init__(self, n, then):
        self.n, self.then = n, then

    def __call__(self):
        self.n -= 1
        if self.n == 0:
            self.then()


def ring(net, n, me, axis, block, size, landed, far):
    reach = n // 2

    def step(way, s):
        part, share = (ALL, 1.0) if s < reach else far[way]
        if part is None:
            return
        ref = block(lax.rem(me - way * (s - 1) + n, n), part)
        to = lax.rem(me + way + n, n)
        net.send(ref, ref, {axis: to}, axis + ("+" if way == 1 else "-"), size * share, lambda: arrived(way, s))

    def arrived(way, s):
        if s < reach:
            step(way, s + 1)
        landed((n - way * s) % n)

    step(1, 1)
    step(-1, 1)


def ring_gather(net, n, me, axis, block, size, done):
    count = Count(n, done)
    ring(net, n, me, axis, block, size, lambda d: count(), {1: (0, 0.5), -1: (1, 0.5)})


def kernel(
    tok,
    gate_left,
    gate_right,
    gate_values,
    gate_rows,
    gate_cols,
    up_left,
    up_right,
    up_values,
    up_rows,
    up_cols,
    grad_hidden,
    table,
    hidden,
    out_gate,
    out_up,
    t_all,
    t_perm,
    t_turn,
    left,
    right,
    shards,
    blocks,
    rank,
    pre,
    chain,
    up_stream,
    dpre,
    back,
    grads,
    came_up,
    came_down,
    leave_up,
    leave_down,
    mine,
    parcels,
    arrived_parcels,
    send_sems,
    recv_sems,
    local_sems,
):
    x, yl, z = lax.axis_index("x"), lax.axis_index("yl"), lax.axis_index("z")
    yh, c = lax.axis_index("yh"), lax.axis_index("c")
    other = 1 - yl

    def round_x(d):
        return lax.rem(x + d + NX, NX)

    def round_z(d):
        return lax.rem(z + d + NZ, NZ)

    pair, twin = {"yl": other}, {"c": 1 - c}
    across, beyond = {"yh": 1 - yh}, {"yh": 1 - yh, "yl": other}
    near = [{"x": round_x(d), "yl": yl if e == 0 else other} for d in range(NX) for e in range(NL)][1:]
    greeted = [twin, across, beyond, {"z": round_z(1)}, {"z": round_z(-1)}, *near]
    barrier = pltpu.get_barrier_semaphore()
    for who in greeted:
        pl.semaphore_signal(barrier, inc=1, device_id=who, device_id_type=pl.DeviceIdType.MESH)

    keeps = []

    def keep(src, dst):
        made = pltpu.make_async_copy(src, dst, local_sems.at[len(keeps)])
        made.start()
        keeps.append(made)

    def cols(ref, which):
        return ref.at[:, pl.ds(pl.multiple_of(which * HALF, BLK), HALF)]

    own_rows = pl.ds(pl.multiple_of(yl * BLK, BLK), BLK)
    other_rows = pl.ds(pl.multiple_of(other * BLK, BLK), BLK)
    keep(cols(gate_right, yl), right.at[x, yl, z, :, 0:HALF])
    keep(cols(up_right, yl), right.at[x, yl, z, :, HALF : 2 * HALF])
    keep(tok, t_all.at[own_rows])
    keep(cols(grad_hidden, yl), up_stream.at[own_rows])
    own_left = pltpu.make_async_copy(gate_left, left.at[x, yl, z], local_sems.at[len(keeps)])

    @pl.when(yl == 0)
    def _():
        own_left.start()

    @pl.when(yl == 1)
    def _():
        pltpu.make_async_copy(up_left, left.at[x, yl, z], local_sems.at[len(keeps)]).start()

    keeps.append(own_left)
    shards[x, yl] = jnp.zeros((2, 32, 2 * BLK), BF16)
    shards[x, yl, 0, 0:KB] = gate_values[...]
    shards[x, yl, 1, 0:KB] = up_values[...]

    pl.semaphore_wait(barrier, len(greeted))
    net = Net(send_sems, recv_sems)

    def do_rank():
        total = jnp.zeros((2 * BLK, TILE), F32)
        for i in range(NX):
            total += dot(t_all[:, i * 1024 : (i + 1) * 1024], left[i].reshape(1024, TILE))
        slot = yl * 4 + yh * 2 + c
        rank[slot] = total.astype(BF16)

    def rank_slot(l, h, core):
        return rank.at[l * 4 + h * 2 + core]

    def share_rank():
        def on(l, h):
            ref = rank_slot(l, h, c)
            net.send(ref, ref, twin, "c", 0.131, rank_there)

        ref = rank_slot(yl, yh, c)
        net.send(ref, ref, pair, "y", 0.131, lambda: on(other, yh))
        net.send(ref, ref, beyond, "y", 0.0, lambda: on(other, 1 - yh))
        net.send(ref, ref, across, "y", 0.0, lambda: on(yl, 1 - yh))
        on(yl, yh)

    def low_rank(first, last):
        def do(j, _):
            g = (j >= 7).astype(jnp.int32)
            at = pl.ds(pl.multiple_of(j * TILE, TILE), TILE)
            total = jnp.zeros((2 * BLK, TILE), F32)
            for i in range(NX):
                total += dot(rank[g * 4 + i], right[i, :, :, :, at].reshape(TILE, TILE))
            pre[j] = total
            return 0

        lax.fori_loop(first, last, do, 0)

    tiles_a, tiles = PART_A // TILE, 2 * HALF // TILE
    product_a = Count(2, lambda: net.work(1.5, lambda: low_rank(0, tiles_a)))
    product_b = Count(2, lambda: net.work(5.0, lambda: low_rank(tiles_a, tiles)))

    def all_ranks():
        product_a()
        product_b()

    rank_there = Count(7 - 3, all_ranks)

    def rank_ready():
        net.work(2.5, do_rank)
        share_rank()

    left_parts = Count(2 + 1, rank_ready)

    def permute_tokens(first, last):
        def do(r, _):
            part = t_all[:, pl.ds(pl.multiple_of(r * BLK, BLK), BLK)]
            new = lax.broadcasted_iota(jnp.int32, (BLK, BLK), 0)
            old = lax.broadcasted_iota(jnp.int32, (BLK, BLK), 1)

            def source(m):
                shard = ((m >> 1) & 3) * 16 + (m & 1) * 8 + (m >> 4)
                return shard * 2 + ((m >> 3) & 1)

            turn = (source(new) == old).astype(F32).astype(BF16)
            straight = (source(old) == new).astype(F32).astype(BF16)
            t_perm[r] = dot(part, straight).astype(BF16)
            t_turn[r] = lax.dot_general(
                turn, part, (((1,), (1,)), ((), ())), preferred_element_type=F32
            ).astype(BF16)
            return 0

        lax.fori_loop(first, last, do, 0)

    def sparse(g, rows_ref, first, last):
        def do(k, _):
            piece = dot(t_perm[rows_ref[k]], blocks[g * KB + k])
            chain[g * 28 + k + 1] = piece + chain[g * 28 + table[g * 64 + k]]
            return 0

        lax.fori_loop(first, last, do, 0)

    def zero_chain():
        chain[0] = jnp.zeros((2 * BLK, BLK), F32)
        chain[28] = jnp.zeros((2 * BLK, BLK), F32)

    def all_sparse():
        net.spare.append((0.2, zero_chain))
        for g, rows_ref in ((0, gate_rows), (1, up_rows)):
            for first in range(0, KB, 9):
                net.spare.append((2.0, lambda a=(g, rows_ref, first, first + 9): sparse(*a)))

    sparse_ready = Count(2, all_sparse)

    def tokens_there():
        left_parts()
        for first in range(0, 32, 8):
            net.spare.append((1.2, lambda a=(first, first + 8): permute_tokens(*a)))
        sparse_ready()

    def spread_values():
        row = lax.broadcasted_iota(jnp.int32, (KB * 16, 512), 0)
        col = lax.broadcasted_iota(jnp.int32, (KB * 16, 512), 1)
        pick = col == (((row >> 3) & 1) * 256 + (row & 7) * 32 + (row >> 4))
        pick = pick.astype(F32).astype(BF16)
        for g in range(2):
            flat = shards[:, :, g].reshape(256, 2 * BLK)
            tall = jnp.concatenate([flat[:, :BLK], flat[:, BLK:]], axis=0)
            laid = dot(pick, tall).astype(BF16).reshape(KB, 16, BLK)
            blocks[g * KB : (g + 1) * KB, pl.ds(pl.multiple_of(z * 16, 16), 16), :] = laid

    def value_slice(i, half):
        some = {0: slice(0, KB), 1: slice(KB, 2 * KB)}.get(half if isinstance(half, int) else None, ALL)
        return blocks.at[some, pl.ds(pl.multiple_of(i * 16, 16), 16), :]

    def values_near():
        net.work(1.5, spread_values)
        ring_gather(net, NZ, z, "z", value_slice, 0.221, sparse_ready)

    def gather(near_a, near_b, far_a, far_b):
        counts_a = [Count(2, lambda d=d: far_a(d)) for d in range(NX)]
        counts_b = [Count(2, lambda d=d: far_b(d)) for d in range(NZ)]

        def begin(half, way):
            far = {way: (ALL, 1.0), -way: (None, 0.0)}
            ref_a, size_a = near_a
            ref_b, size_b = near_b
            ring(net, NX, x, "x", lambda i, _: ref_a(i, half), size_a, lambda d: counts_a[d](), far)
            ring(net, NZ, z, "z", lambda i, _: ref_b(i, half), size_b, lambda d: counts_b[d](), far)
            counts_a[0]()
            counts_b[0]()

        return (lambda: begin(yl, 1)), (lambda: begin(other, -1))

    def left_gather():
        a, b = slice(0, 32), slice(32, 64)

        def a_far():
            ring_gather(net, NZ, z, "z", lambda i, h: left.at[:, h, i, a], 0.131, left_parts)

        def b_far():
            ring_gather(net, NX, x, "x", lambda i, h: left.at[i, h, :, b], 0.262, left_parts)

        all_a, all_b = Count(NX, a_far), Count(NZ, b_far)
        return gather(
            (lambda i, h: left.at[i, h, z, a], 0.016),
            (lambda i, h: left.at[x, h, i, b], 0.016),
            lambda d: all_a(),
            lambda d: all_b(),
        )

    def right_gather():
        a, b = slice(0, PART_A), slice(PART_A, 2 * HALF)
        size_a, size_b = PART_A * 64e-6, (2 * HALF - PART_A) * 64e-6
        all_a, all_b = Count(NX, product_a), Count(NZ, product_b)

        def a_far(d):
            i = round_x(d)
            ring_gather(net, NZ, z, "z", lambda k, h: right.at[i, h, k, :, a], size_a, all_a)

        def b_far(d):
            i = round_z(d)
            ring_gather(net, NX, x, "x", lambda k, h: right.at[k, h, i, :, b], size_b, all_b)

        return gather(
            (lambda i, h: right.at[i, h, z, :, a], size_a / 2),
            (lambda i, h: right.at[x, h, i, :, b], size_b / 2),
            a_far,
            b_far,
        )

    swap_left = net.copy(up_left, left.at[x, yl, z], pair)

    @pl.when(yl == 0)
    def _():
        swap_left.start()

    @pl.when(yl == 1)
    def _():
        net.copy(gate_left, left.at[x, yl, z], pair).start()

    for made in keeps:
        made.wait()
    left_own, left_other = left_gather()
    right_own, right_other = right_gather()
    net.track(swap_left, "y", 0.033, left_other)
    swapped_right = Count(2, right_other)
    net.send(cols(gate_right, other), right.at[x, yl, z, :, 0:HALF], pair, "y", 0.057, swapped_right)
    net.send(
        cols(up_right, other), right.at[x, yl, z, :, HALF : 2 * HALF], pair, "y", 0.057, swapped_right
    )
    net.send(
        shards.at[x, yl],
        shards.at[x, yl],
        pair,
        "y",
        0.033,
        lambda: ring_gather(net, NX, x, "x", lambda i, h: shards.at[i, h], 0.066, values_near),
    )
    mine_half = pl.ds(pl.multiple_of(c * 64, 64), 64)
    sent_half = pl.ds(pl.multiple_of(yl * BLK + c * 64, 64), 64)
    got_half = pl.ds(pl.multiple_of(other * BLK + c * 64, 64), 64)
    net.send(
        tok.at[mine_half],
        t_all.at[sent_half],
        pair,
        "y",
        0.524,
        lambda: net.send(t_all.at[got_half], t_all.at[got_half], twin, "c", 0.524, tokens_there),
    )
    net.send(cols(grad_hidden, other), up_stream.at[own_rows], pair, "y", 0.459, lambda: None)
    left_own()
    right_own()
    net.run()

    def gated(j, _):
        for h in range(2):
            for rows, mine_too in ((other_rows, False), (own_rows, True)):
                lanes = slice(h * BLK, (h + 1) * BLK)
                col = j * 2 + h
                gate = pre[j, rows, lanes] + chain[table[32 + yl * 14 + col], rows, :]
                up = pre[7 + j, rows, lanes] + chain[28 + table[96 + yl * 14 + col], rows, :]
                coming = up_stream[rows, pl.ds(pl.multiple_of(col * BLK, BLK), BLK)].astype(F32)
                sigma = jax.nn.sigmoid(gate)
                silu = gate * sigma
                unit = (silu * up).astype(BF16)
                dpre[col, rows, :] = (coming * up * sigma * (1.0 + gate * (1.0 - sigma))).astype(BF16)
                dpre[14 + col, rows, :] = (coming * silu).astype(BF16)
                if mine_too:
                    hidden[:, pl.ds(pl.multiple_of(yl * HALF + col * BLK, BLK), BLK)] = unit
                else:
                    back[:, pl.ds(pl.multiple_of(col * BLK, BLK), BLK)] = unit
        return 0

    lax.fori_loop(0, 7, gated, 0)
    net.send(back, cols(hidden, yl), pair, "y", 0.459, lambda: None)

    for g, rows_ref, cols_ref in ((0, gate_rows, gate_cols), (1, up_rows, up_cols)):

        def gradient(k, _, g=g, rows_ref=rows_ref, cols_ref=cols_ref):
            col = cols_ref[k] - (yh * 2 + c) * 28 - yl * 14
            inside = (col >= 0) & (col < 14)
            term = dot(t_turn[rows_ref[k]], dpre[g * 14 + jnp.clip(col, 0, 13)])
            grads[g * KB + k] = jnp.where(inside, term, 0.0)
            return 0

        lax.fori_loop(0, KB, gradient, 0)

    def lot(i):
        return pl.ds(pl.multiple_of(i * 16, 16), 16)

    def exchange():
        total = grads[:, lot(z), :] + came_up[3].astype(F32) + came_down[3].astype(F32)
        mine[...] = total.reshape(2 * KB * 16, BLK)
        for s in range(8):
            for g in range(2):
                for p in range(2):
                    rows = pl.ds(g * KB * 16 + p * 8 + s, KB, stride=16)
                    parcels[s, g * 32 : g * 32 + KB, p * BLK : (p + 1) * BLK] = mine[rows, :]
        for d in range(NX):
            for e in range(NL):
                if d == 0 and e == 0:
                    continue
                to_x, to_l = round_x(d), (yl if e == 0 else other)
                net.send(
                    parcels.at[to_x * 2 + to_l],
                    arrived_parcels.at[d * 2 + e],
                    {"x": to_x, "yl": to_l},
                    "x+",
                    0.065,
                    lambda: None,
                )

    home = Count(2, exchange)

    def pass_on(way, j):
        came, leaves = (came_up, leave_up) if way == 1 else (came_down, leave_down)
        at = lot(round_z(way * (5 - j)))
        first, last = (0, 2 * KB) if j > 1 else ((0, KB) if way == 1 else (KB, 2 * KB))
        if j == 2:
            half, rest = (slice(0, KB), slice(KB, 2 * KB))[::way]
            leaves[1, half] = (grads[half, at, :] + came[0, half].astype(F32)).astype(BF16)
            leaves[1, rest] = grads[rest, at, :].astype(BF16)
        elif j > 2:
            leaves[j - 1] = (grads[:, at, :] + came[j - 2].astype(F32)).astype(BF16)
        else:
            leaves[0, first:last] = grads[first:last, at, :].astype(BF16)
        net.send(
            leaves.at[j - 1, first:last],
            came.at[j - 1, first:last],
            {"z": round_z(way)},
            "z+" if way == 1 else "z-",
            0.11 if j == 1 else 0.221,
            lambda: home() if j == 4 else pass_on(way, j + 1),
        )

    pass_on(1, 1)
    pass_on(-1, 1)
    net.run()
    total = parcels[x * 2 + yl]
    for i in range(1, 8):
        total = total + arrived_parcels[i]
    out_gate[...] = total[0:KB]
    out_up[...] = total[32 : 32 + KB]
    net.finish()


def chains(gate_cols, up_cols, base):
    cols = jnp.stack([gate_cols, up_cols]) - base
    index = jnp.arange(64, dtype=jnp.int32)
    padded = jnp.pad(cols, ((0, 0), (0, 64 - KB)))
    asked = jnp.where(index < 32, padded, index - 32)
    limit = jnp.where(index < 32, index, KB)
    earlier = jnp.arange(KB, dtype=jnp.int32)
    hit = (cols[:, None, :] == asked[:, :, None]) & (earlier < limit[:, None])
    return jnp.max(jnp.where(hit, earlier + 1, 0), axis=2).reshape(128)


def on_device(*args):
    base = (lax.axis_index("yh") * 2 + lax.axis_index("c")) * 28
    table = chains(args[5], args[10], base)
    vmem, smem = pl.BlockSpec(memory_space=pltpu.VMEM), pl.BlockSpec(memory_space=pltpu.SMEM)
    specs = [vmem, vmem, vmem, vmem, smem, smem, vmem, vmem, vmem, smem, smem, vmem, smem]
    copies = 176
    return pl.pallas_call(
        kernel,
        out_shape=(
            jax.ShapeDtypeStruct((BLK, 2 * HALF), BF16),
            jax.ShapeDtypeStruct((KB, 2 * BLK), F32),
            jax.ShapeDtypeStruct((KB, 2 * BLK), F32),
        ),
        in_specs=specs,
        out_specs=(vmem, vmem, vmem),
        scratch_shapes=[
            pltpu.VMEM((2 * BLK, 4096), BF16),
            pltpu.VMEM((32, 2 * BLK, BLK), BF16),
            pltpu.VMEM((32, BLK, 2 * BLK), BF16),
            pltpu.VMEM((NX, NL, NZ, 64, TILE), BF16),
            pltpu.VMEM((NX, NL, NZ, 16, 2 * HALF), BF16),
            pltpu.VMEM((NX, NL, 2, 32, 2 * BLK), BF16),
            pltpu.VMEM((2 * KB, BLK, BLK), BF16),
            pltpu.VMEM((8, 2 * BLK, TILE), BF16),
            pltpu.VMEM((14, 2 * BLK, TILE), F32),
            pltpu.VMEM((56, 2 * BLK, BLK), F32),
            pltpu.VMEM((2 * BLK, HALF), BF16),
            pltpu.VMEM((28, 2 * BLK, BLK), BF16),
            pltpu.VMEM((BLK, HALF), BF16),
            pltpu.VMEM((2 * KB, BLK, BLK), F32),
            pltpu.VMEM((4, 2 * KB, 16, BLK), BF16),
            pltpu.VMEM((4, 2 * KB, 16, BLK), BF16),
            pltpu.VMEM((4, 2 * KB, 16, BLK), BF16),
            pltpu.VMEM((4, 2 * KB, 16, BLK), BF16),
            pltpu.VMEM((2 * KB * 16, BLK), F32),
            pltpu.VMEM((8, 64, 2 * BLK), F32),
            pltpu.VMEM((8, 64, 2 * BLK), F32),
            pltpu.SemaphoreType.DMA((copies,)),
            pltpu.SemaphoreType.DMA((copies,)),
            pltpu.SemaphoreType.DMA((8,)),
        ],
        compiler_params=pltpu.CompilerParams(
            collective_id=0, has_side_effects=True, vmem_limit_bytes=58 * 2**20
        ),
    )(*args, table)


def solution(mesh):
    finer = Mesh(mesh.devices.reshape(NX, NL, NZ, NH, NC), (*FSDP, *TP))
    return jax.shard_map(
        on_device,
        mesh=finer,
        in_specs=(
            P(FSDP, None),
            P(FSDP, TP),
            P(FSDP, TP),
            P(TP, FSDP),
            P(TP),
            P(TP),
            P(FSDP, TP),
            P(FSDP, TP),
            P(TP, FSDP),
            P(TP),
            P(TP),
            P(FSDP, TP),
        ),
        out_specs=(P(FSDP, TP), P(TP, FSDP), P(TP, FSDP)),
        check_vma=False,
    )
```

```python
import heapq

import jax
import jax.numpy as jnp
from jax import lax
from jax.experimental import pallas as pl
from jax.experimental.pallas import tpu as pltpu
from jax.sharding import Mesh
from jax.sharding import PartitionSpec as P

BLK = 128
NX, NL, NZ, NH, NC = 4, 2, 8, 2, 2
FSDP = ("x", "yl", "z")
TP = ("yh", "c")
KB = 27
HALF = 1792
TILE = 256
PART_A = 768
ALL = slice(None)
NEAR, VALUES, FAR = 1, 1, 2
F32, BF16 = jnp.float32, jnp.bfloat16


def dot(a, b):
    return jnp.dot(a, b, preferred_element_type=F32)


class Net:
    LATENCY, WINDOW = 3.0, 5.0
    RATE = {"x+": 0.045, "x-": 0.045, "z+": 0.045, "z-": 0.045, "y": 0.045, "c": 0.2, "owner": 0.1}

    def __init__(self, send_sems, recv_sems):
        self.sems = (send_sems, recv_sems)
        self.now, self.free, self.heap, self.copies, self.spare = 0.0, {}, [], [], []
        self.waiting, self.asked = {}, 0

    def copy(self, src, dst, where):
        i = len(self.copies)
        made = pltpu.make_async_remote_copy(
            src_ref=src,
            dst_ref=dst,
            send_sem=self.sems[0].at[i],
            recv_sem=self.sems[1].at[i],
            device_id=where,
            device_id_type=pl.DeviceIdType.MESH,
        )
        return made

    def track(self, made, link, size, then):
        self.copies.append(made)
        begin = max(self.now, self.free.get(link, 0.0))
        self.free[link] = begin + size / self.RATE[link]
        heapq.heappush(self.heap, (self.free[link] + self.LATENCY, len(self.copies), made, then))

    def send(self, src, dst, where, link, size, then, urgency=0):
        self.asked += 1
        order = (urgency, self.asked)
        heapq.heappush(self.waiting.setdefault(link, []), (order, src, dst, where, size, then))
        self.issue()

    def issue(self):
        for link, queue in self.waiting.items():
            while queue and self.free.get(link, 0.0) < self.now + self.WINDOW:
                _, src, dst, where, size, then = heapq.heappop(queue)
                made = self.copy(src, dst, where)
                made.start()
                self.track(made, link, size, then)

    def work(self, cost, do):
        do()
        self.now += cost
        self.issue()

    def run(self):
        turn = 0
        while self.heap:
            at, _, made, then = heapq.heappop(self.heap)
            if self.spare and (turn % 2 or self.now + self.spare[0][0] <= at + 0.5):
                self.work(*self.spare.pop(0))
            turn += 1
            self.now = max(self.now, at)
            made.wait_recv()
            then()
            self.issue()
        while self.spare:
            self.work(*self.spare.pop(0))

    def finish(self):
        for made in self.copies:
            made.wait_send()


class Count:
    def __init__(self, n, then):
        self.n, self.then = n, then

    def __call__(self):
        self.n -= 1
        if self.n == 0:
            self.then()


def ring(net, n, me, axis, block, size, landed, far, urgency):
    reach = n // 2

    def step(way, s):
        part, share = (ALL, 1.0) if s < reach else far[way]
        if part is None:
            return
        ref = block(lax.rem(me - way * (s - 1) + n, n), part)
        to = lax.rem(me + way + n, n)
        net.send(ref, ref, {axis: to}, axis + ("+" if way == 1 else "-"), size * share, lambda: arrived(way, s), urgency)

    def arrived(way, s):
        if s < reach:
            step(way, s + 1)
        landed((n - way * s) % n)

    step(1, 1)
    step(-1, 1)


def ring_gather(net, n, me, axis, block, size, done, urgency=0):
    count = Count(n, done)
    ring(net, n, me, axis, block, size, lambda d: count(), {1: (0, 0.5), -1: (1, 0.5)}, urgency)


def kernel(
    tok,
    gate_left,
    gate_right,
    gate_values,
    gate_rows,
    gate_cols,
    up_left,
    up_right,
    up_values,
    up_rows,
    up_cols,
    grad_hidden,
    table,
    hidden,
    out_gate,
    out_up,
    t_all,
    t_perm,
    t_turn,
    left,
    right,
    shards,
    blocks,
    rank,
    pre,
    chain,
    up_stream,
    dpre,
    back,
    grads,
    came_up,
    came_down,
    leave_up,
    leave_down,
    mine,
    parcels,
    arrived_parcels,
    send_sems,
    recv_sems,
    local_sems,
):
    x, yl, z = lax.axis_index("x"), lax.axis_index("yl"), lax.axis_index("z")
    yh, c = lax.axis_index("yh"), lax.axis_index("c")
    other = 1 - yl

    def round_x(d):
        return lax.rem(x + d + NX, NX)

    def round_z(d):
        return lax.rem(z + d + NZ, NZ)

    pair, twin = {"yl": other}, {"c": 1 - c}
    across, beyond = {"yh": 1 - yh}, {"yh": 1 - yh, "yl": other}
    near = [{"x": round_x(d), "yl": yl if e == 0 else other} for d in range(NX) for e in range(NL)][1:]
    greeted = [twin, across, beyond, {"z": round_z(1)}, {"z": round_z(-1)}, *near]
    barrier = pltpu.get_barrier_semaphore()
    for who in greeted:
        pl.semaphore_signal(barrier, inc=1, device_id=who, device_id_type=pl.DeviceIdType.MESH)

    keeps = []

    def keep(src, dst):
        made = pltpu.make_async_copy(src, dst, local_sems.at[len(keeps)])
        made.start()
        keeps.append(made)

    def cols(ref, which):
        return ref.at[:, pl.ds(pl.multiple_of(which * HALF, BLK), HALF)]

    own_rows = pl.ds(pl.multiple_of(yl * BLK, BLK), BLK)
    other_rows = pl.ds(pl.multiple_of(other * BLK, BLK), BLK)
    keep(cols(gate_right, yl), right.at[x, yl, z, :, 0:HALF])
    keep(cols(up_right, yl), right.at[x, yl, z, :, HALF : 2 * HALF])
    keep(tok, t_all.at[own_rows])
    keep(cols(grad_hidden, yl), up_stream.at[own_rows])
    own_left = pltpu.make_async_copy(gate_left, left.at[x, yl, z], local_sems.at[len(keeps)])

    @pl.when(yl == 0)
    def _():
        own_left.start()

    @pl.when(yl == 1)
    def _():
        pltpu.make_async_copy(up_left, left.at[x, yl, z], local_sems.at[len(keeps)]).start()

    keeps.append(own_left)
    shards[x, yl] = jnp.zeros((2, 32, 2 * BLK), BF16)
    shards[x, yl, 0, 0:KB] = gate_values[...]
    shards[x, yl, 1, 0:KB] = up_values[...]

    pl.semaphore_wait(barrier, len(greeted))
    net = Net(send_sems, recv_sems)

    def do_rank():
        total = jnp.zeros((2 * BLK, TILE), F32)
        for i in range(NX):
            total += dot(t_all[:, i * 1024 : (i + 1) * 1024], left[i].reshape(1024, TILE))
        slot = yl * 4 + yh * 2 + c
        rank[slot] = total.astype(BF16)

    def rank_slot(l, h, core):
        return rank.at[l * 4 + h * 2 + core]

    def share_rank():
        def on(l, h):
            ref = rank_slot(l, h, c)
            net.send(ref, ref, twin, "c", 0.131, rank_there)

        ref = rank_slot(yl, yh, c)
        net.send(ref, ref, pair, "y", 0.131, lambda: on(other, yh))
        net.send(ref, ref, beyond, "y", 0.0, lambda: on(other, 1 - yh))
        net.send(ref, ref, across, "y", 0.0, lambda: on(yl, 1 - yh))
        on(yl, yh)

    def low_rank(first, last):
        def do(j, _):
            g = (j >= 7).astype(jnp.int32)
            at = pl.ds(pl.multiple_of(j * TILE, TILE), TILE)
            total = jnp.zeros((2 * BLK, TILE), F32)
            for i in range(NX):
                total += dot(rank[g * 4 + i], right[i, :, :, :, at].reshape(TILE, TILE))
            pre[j] = total
            return 0

        lax.fori_loop(first, last, do, 0)

    tiles_a, tiles = PART_A // TILE, 2 * HALF // TILE
    product_a = Count(2, lambda: net.work(0.6, lambda: low_rank(0, tiles_a)))
    product_b = Count(2, lambda: net.work(2.0, lambda: low_rank(tiles_a, tiles)))

    def all_ranks():
        product_a()
        product_b()

    rank_there = Count(7 - 3, all_ranks)

    def rank_ready():
        net.work(1.0, do_rank)
        share_rank()

    left_parts = Count(2 + 1, rank_ready)

    def permute_tokens(first, last):
        def do(r, _):
            part = t_all[:, pl.ds(pl.multiple_of(r * BLK, BLK), BLK)]
            new = lax.broadcasted_iota(jnp.int32, (BLK, BLK), 0)
            old = lax.broadcasted_iota(jnp.int32, (BLK, BLK), 1)

            def source(m):
                shard = ((m >> 1) & 3) * 16 + (m & 1) * 8 + (m >> 4)
                return shard * 2 + ((m >> 3) & 1)

            turn = (source(new) == old).astype(F32).astype(BF16)
            straight = (source(old) == new).astype(F32).astype(BF16)
            t_perm[r] = dot(part, straight).astype(BF16)
            t_turn[r] = lax.dot_general(
                turn, part, (((1,), (1,)), ((), ())), preferred_element_type=F32
            ).astype(BF16)
            return 0

        lax.fori_loop(first, last, do, 0)

    def sparse(g, rows_ref, first, last):
        def do(k, _):
            piece = dot(t_perm[rows_ref[k]], blocks[g * KB + k])
            chain[g * 28 + k + 1] = piece + chain[g * 28 + table[g * 64 + k]]
            return 0

        lax.fori_loop(first, last, do, 0)

    def zero_chain():
        chain[0] = jnp.zeros((2 * BLK, BLK), F32)
        chain[28] = jnp.zeros((2 * BLK, BLK), F32)

    def all_sparse():
        net.spare.append((0.2, zero_chain))
        for g, rows_ref in ((0, gate_rows), (1, up_rows)):
            for first in range(0, KB, 9):
                net.spare.append((0.5, lambda a=(g, rows_ref, first, first + 9): sparse(*a)))

    sparse_ready = Count(2, all_sparse)

    def tokens_there():
        left_parts()
        for first in range(0, 32, 8):
            net.spare.append((0.4, lambda a=(first, first + 8): permute_tokens(*a)))
        sparse_ready()

    def spread_values():
        row = lax.broadcasted_iota(jnp.int32, (KB * 16, 512), 0)
        col = lax.broadcasted_iota(jnp.int32, (KB * 16, 512), 1)
        pick = col == (((row >> 3) & 1) * 256 + (row & 7) * 32 + (row >> 4))
        pick = pick.astype(F32).astype(BF16)
        for g in range(2):
            flat = shards[:, :, g].reshape(256, 2 * BLK)
            tall = jnp.concatenate([flat[:, :BLK], flat[:, BLK:]], axis=0)
            laid = dot(pick, tall).astype(BF16).reshape(KB, 16, BLK)
            blocks[g * KB : (g + 1) * KB, pl.ds(pl.multiple_of(z * 16, 16), 16), :] = laid

    def value_slice(i, half):
        some = {0: slice(0, KB), 1: slice(KB, 2 * KB)}.get(half if isinstance(half, int) else None, ALL)
        return blocks.at[some, pl.ds(pl.multiple_of(i * 16, 16), 16), :]

    def values_near():
        net.work(1.0, spread_values)
        ring_gather(net, NZ, z, "z", value_slice, 0.221, sparse_ready, VALUES)

    def gather(near_a, near_b, far_a, far_b, urgency):
        counts_a = [Count(2, lambda d=d: far_a(d)) for d in range(NX)]
        counts_b = [Count(2, lambda d=d: far_b(d)) for d in range(NZ)]

        def begin(half, way):
            far = {way: (ALL, 1.0), -way: (None, 0.0)}
            ref_a, size_a = near_a
            ref_b, size_b = near_b
            ring(net, NX, x, "x", lambda i, _: ref_a(i, half), size_a, lambda d: counts_a[d](), far, urgency)
            ring(net, NZ, z, "z", lambda i, _: ref_b(i, half), size_b, lambda d: counts_b[d](), far, urgency)
            counts_a[0]()
            counts_b[0]()

        return (lambda: begin(yl, 1)), (lambda: begin(other, -1))

    def left_gather():
        a, b = slice(0, 32), slice(32, 64)
        all_a, all_b = Count(NX, left_parts), Count(NZ, left_parts)

        def a_far(d):
            i = round_x(d)
            ring_gather(net, NZ, z, "z", lambda k, h: left.at[i, h, k, a], 0.033, all_a)

        def b_far(d):
            i = round_z(d)
            ring_gather(net, NX, x, "x", lambda k, h: left.at[k, h, i, b], 0.033, all_b)

        return gather(
            (lambda i, h: left.at[i, h, z, a], 0.016),
            (lambda i, h: left.at[x, h, i, b], 0.016),
            a_far,
            b_far,
            0,
        )

    def right_gather():
        a, b = slice(0, PART_A), slice(PART_A, 2 * HALF)
        size_a, size_b = PART_A * 64e-6, (2 * HALF - PART_A) * 64e-6
        all_a, all_b = Count(NX, product_a), Count(NZ, product_b)

        def a_far(d):
            i = round_x(d)
            ring_gather(net, NZ, z, "z", lambda k, h: right.at[i, h, k, :, a], size_a, all_a, FAR)

        def b_far(d):
            i = round_z(d)
            ring_gather(net, NX, x, "x", lambda k, h: right.at[k, h, i, :, b], size_b, all_b, FAR)

        return gather(
            (lambda i, h: right.at[i, h, z, :, a], size_a / 2),
            (lambda i, h: right.at[x, h, i, :, b], size_b / 2),
            a_far,
            b_far,
            NEAR,
        )

    swap_left = net.copy(up_left, left.at[x, yl, z], pair)

    @pl.when(yl == 0)
    def _():
        swap_left.start()

    @pl.when(yl == 1)
    def _():
        net.copy(gate_left, left.at[x, yl, z], pair).start()

    for made in keeps:
        made.wait()
    left_own, left_other = left_gather()
    right_own, right_other = right_gather()
    net.track(swap_left, "y", 0.033, left_other)
    swapped_right = Count(2, right_other)
    net.send(cols(gate_right, other), right.at[x, yl, z, :, 0:HALF], pair, "y", 0.057, swapped_right)
    net.send(
        cols(up_right, other), right.at[x, yl, z, :, HALF : 2 * HALF], pair, "y", 0.057, swapped_right
    )
    net.send(
        shards.at[x, yl],
        shards.at[x, yl],
        pair,
        "y",
        0.033,
        lambda: ring_gather(net, NX, x, "x", lambda i, h: shards.at[i, h], 0.066, values_near, 1),
    )
    mine_half = pl.ds(pl.multiple_of(c * 64, 64), 64)
    sent_half = pl.ds(pl.multiple_of(yl * BLK + c * 64, 64), 64)
    got_half = pl.ds(pl.multiple_of(other * BLK + c * 64, 64), 64)
    net.send(
        tok.at[mine_half],
        t_all.at[sent_half],
        pair,
        "y",
        0.524,
        lambda: net.send(t_all.at[got_half], t_all.at[got_half], twin, "c", 0.524, tokens_there),
    )
    net.send(cols(grad_hidden, other), up_stream.at[own_rows], pair, "y", 0.459, lambda: None)
    left_own()
    right_own()
    net.run()

    def gated(j, _):
        for h in range(2):
            for rows, mine_too in ((other_rows, False), (own_rows, True)):
                lanes = slice(h * BLK, (h + 1) * BLK)
                col = j * 2 + h
                gate = pre[j, rows, lanes] + chain[table[32 + yl * 14 + col], rows, :]
                up = pre[7 + j, rows, lanes] + chain[28 + table[96 + yl * 14 + col], rows, :]
                coming = up_stream[rows, pl.ds(pl.multiple_of(col * BLK, BLK), BLK)].astype(F32)
                sigma = jax.nn.sigmoid(gate)
                silu = gate * sigma
                unit = (silu * up).astype(BF16)
                dpre[col, rows, :] = (coming * up * sigma * (1.0 + gate * (1.0 - sigma))).astype(BF16)
                dpre[14 + col, rows, :] = (coming * silu).astype(BF16)
                if mine_too:
                    hidden[:, pl.ds(pl.multiple_of(yl * HALF + col * BLK, BLK), BLK)] = unit
                else:
                    back[:, pl.ds(pl.multiple_of(col * BLK, BLK), BLK)] = unit
        return 0

    lax.fori_loop(0, 7, gated, 0)
    net.send(back, cols(hidden, yl), pair, "y", 0.459, lambda: None)

    def lot(i):
        return pl.ds(pl.multiple_of(i * 16, 16), 16)

    def to_owners(g):
        these = slice(g * KB, (g + 1) * KB)
        total = grads[these, lot(z), :] + came_up[3, these].astype(F32) + came_down[3, these].astype(F32)
        mine[g] = total.reshape(KB * 16, BLK)
        for s in range(8):
            for p in range(2):
                parcels[s, g, 0:KB, p * BLK : (p + 1) * BLK] = mine[g, pl.ds(p * 8 + s, KB, stride=16), :]
        for d in range(NX):
            for e in range(NL):
                if d == 0 and e == 0:
                    continue
                to_x, to_l = round_x(d), (yl if e == 0 else other)
                net.send(
                    parcels.at[to_x * 2 + to_l, g],
                    arrived_parcels.at[d * 2 + e, g],
                    {"x": to_x, "yl": to_l},
                    "owner",
                    0.033,
                    lambda: None,
                )

    def sum_round_z(g):
        begin, middle, end = g * KB, g * KB + 14, (g + 1) * KB
        home = Count(2, lambda: to_owners(g))

        def pass_on(way, j):
            came, leaves = (came_up, leave_up) if way == 1 else (came_down, leave_down)
            at = lot(round_z(way * (5 - j)))
            half, rest = (slice(begin, middle), slice(middle, end))[::way]
            these = half if j == 1 else slice(begin, end)
            if j == 1:
                leaves[0, half] = grads[half, at, :].astype(BF16)
            elif j == 2:
                leaves[1, half] = (grads[half, at, :] + came[0, half].astype(F32)).astype(BF16)
                leaves[1, rest] = grads[rest, at, :].astype(BF16)
            else:
                leaves[j - 1, these] = (grads[these, at, :] + came[j - 2, these].astype(F32)).astype(BF16)
            net.send(
                leaves.at[j - 1, these],
                came.at[j - 1, these],
                {"z": round_z(way)},
                "z+" if way == 1 else "z-",
                0.055 if j == 1 else 0.11,
                lambda: home() if j == 4 else pass_on(way, j + 1),
            )

        pass_on(1, 1)
        pass_on(-1, 1)

    for g, rows_ref, cols_ref in ((0, gate_rows, gate_cols), (1, up_rows, up_cols)):

        def gradient(k, _, g=g, rows_ref=rows_ref, cols_ref=cols_ref):
            col = cols_ref[k] - (yh * 2 + c) * 28 - yl * 14
            inside = (col >= 0) & (col < 14)
            term = dot(t_turn[rows_ref[k]], dpre[g * 14 + jnp.clip(col, 0, 13)])
            grads[g * KB + k] = jnp.where(inside, term, 0.0)
            return 0

        lax.fori_loop(0, KB, gradient, 0)
        sum_round_z(g)
        net.now += 1.0
    net.run()
    total = parcels[x * 2 + yl]
    for i in range(1, 8):
        total = total + arrived_parcels[i]
    out_gate[...] = total[0, 0:KB]
    out_up[...] = total[1, 0:KB]
    net.finish()


def chains(gate_cols, up_cols, base):
    cols = jnp.stack([gate_cols, up_cols]) - base
    index = jnp.arange(64, dtype=jnp.int32)
    padded = jnp.pad(cols, ((0, 0), (0, 64 - KB)))
    asked = jnp.where(index < 32, padded, index - 32)
    limit = jnp.where(index < 32, index, KB)
    earlier = jnp.arange(KB, dtype=jnp.int32)
    hit = (cols[:, None, :] == asked[:, :, None]) & (earlier < limit[:, None])
    return jnp.max(jnp.where(hit, earlier + 1, 0), axis=2).reshape(128)


def on_device(*args):
    base = (lax.axis_index("yh") * 2 + lax.axis_index("c")) * 28
    table = chains(args[5], args[10], base)
    vmem, smem = pl.BlockSpec(memory_space=pltpu.VMEM), pl.BlockSpec(memory_space=pltpu.SMEM)
    specs = [vmem, vmem, vmem, vmem, smem, smem, vmem, vmem, vmem, smem, smem, vmem, smem]
    copies = 240
    return pl.pallas_call(
        kernel,
        out_shape=(
            jax.ShapeDtypeStruct((BLK, 2 * HALF), BF16),
            jax.ShapeDtypeStruct((KB, 2 * BLK), F32),
            jax.ShapeDtypeStruct((KB, 2 * BLK), F32),
        ),
        in_specs=specs,
        out_specs=(vmem, vmem, vmem),
        scratch_shapes=[
            pltpu.VMEM((2 * BLK, 4096), BF16),
            pltpu.VMEM((32, 2 * BLK, BLK), BF16),
            pltpu.VMEM((32, BLK, 2 * BLK), BF16),
            pltpu.VMEM((NX, NL, NZ, 64, TILE), BF16),
            pltpu.VMEM((NX, NL, NZ, 16, 2 * HALF), BF16),
            pltpu.VMEM((NX, NL, 2, 32, 2 * BLK), BF16),
            pltpu.VMEM((2 * KB, BLK, BLK), BF16),
            pltpu.VMEM((8, 2 * BLK, TILE), BF16),
            pltpu.VMEM((14, 2 * BLK, TILE), F32),
            pltpu.VMEM((56, 2 * BLK, BLK), F32),
            pltpu.VMEM((2 * BLK, HALF), BF16),
            pltpu.VMEM((28, 2 * BLK, BLK), BF16),
            pltpu.VMEM((BLK, HALF), BF16),
            pltpu.VMEM((2 * KB, BLK, BLK), F32),
            pltpu.VMEM((4, 2 * KB, 16, BLK), BF16),
            pltpu.VMEM((4, 2 * KB, 16, BLK), BF16),
            pltpu.VMEM((4, 2 * KB, 16, BLK), BF16),
            pltpu.VMEM((4, 2 * KB, 16, BLK), BF16),
            pltpu.VMEM((2, KB * 16, BLK), F32),
            pltpu.VMEM((8, 2, 32, 2 * BLK), F32),
            pltpu.VMEM((8, 2, 32, 2 * BLK), F32),
            pltpu.SemaphoreType.DMA((copies,)),
            pltpu.SemaphoreType.DMA((copies,)),
            pltpu.SemaphoreType.DMA((8,)),
        ],
        compiler_params=pltpu.CompilerParams(
            collective_id=0, has_side_effects=True, vmem_limit_bytes=58 * 2**20
        ),
    )(*args, table)


def solution(mesh):
    finer = Mesh(mesh.devices.reshape(NX, NL, NZ, NH, NC), (*FSDP, *TP))
    return jax.shard_map(
        on_device,
        mesh=finer,
        in_specs=(
            P(FSDP, None),
            P(FSDP, TP),
            P(FSDP, TP),
            P(TP, FSDP),
            P(TP),
            P(TP),
            P(FSDP, TP),
            P(FSDP, TP),
            P(TP, FSDP),
            P(TP),
            P(TP),
            P(FSDP, TP),
        ),
        out_specs=(P(FSDP, TP), P(TP, FSDP), P(TP, FSDP)),
        check_vma=False,
    )
```

```python
import heapq

import jax
import jax.numpy as jnp
from jax import lax
from jax.experimental import pallas as pl
from jax.experimental.pallas import tpu as pltpu
from jax.sharding import Mesh
from jax.sharding import PartitionSpec as P

BLK = 128
NX, NL, NZ, NH, NC = 4, 2, 8, 2, 2
FSDP = ("x", "yl", "z")
TP = ("yh", "c")
KB = 27
HALF = 1792
TILE = 256
PARTS = ((0, 512), (512, 1280), (1280, 1792))
LEFT_A = 16
ALL = slice(None)
WIDE, MIDDLE, TIGHT = 50.0, 8.0, 3.0
NEAR, VALUES, FAR, LATE = 1, 1, 2, 3
F32, BF16 = jnp.float32, jnp.bfloat16


def dot(a, b):
    return jnp.dot(a, b, preferred_element_type=F32)


class Net:
    LATENCY = 3.0
    RATE = {"x+": 0.045, "x-": 0.045, "z+": 0.045, "z-": 0.045, "y": 0.045, "c": 0.2, "owner": 0.1}

    def __init__(self, send_sems, recv_sems):
        self.sems = (send_sems, recv_sems)
        self.now, self.free, self.heap, self.copies, self.spare = 0.0, {}, [], [], []
        self.waiting, self.asked = {}, 0
        self.window = {0: WIDE, 1: MIDDLE, 2: TIGHT, 3: TIGHT}

    def copy(self, src, dst, where):
        i = len(self.copies)
        made = pltpu.make_async_remote_copy(
            src_ref=src,
            dst_ref=dst,
            send_sem=self.sems[0].at[i],
            recv_sem=self.sems[1].at[i],
            device_id=where,
            device_id_type=pl.DeviceIdType.MESH,
        )
        return made

    def track(self, made, link, size, then):
        self.copies.append(made)
        begin = max(self.now, self.free.get(link, 0.0))
        self.free[link] = begin + size / self.RATE[link]
        heapq.heappush(self.heap, (self.free[link] + self.LATENCY, len(self.copies), made, then))

    def send(self, src, dst, where, link, size, then, urgency=0):
        self.asked += 1
        order = (urgency, self.asked)
        heapq.heappush(self.waiting.setdefault(link, []), (order, src, dst, where, size, then))
        self.issue()

    def issue(self):
        for link, queue in self.waiting.items():
            while queue and self.free.get(link, 0.0) < self.now + self.window[queue[0][0][0]]:
                _, src, dst, where, size, then = heapq.heappop(queue)
                made = self.copy(src, dst, where)
                made.start()
                self.track(made, link, size, then)

    def work(self, cost, do):
        do()
        self.now += cost
        self.issue()

    def run(self):
        turn = 0
        while self.heap:
            at, _, made, then = heapq.heappop(self.heap)
            if self.spare and (turn % 2 or self.now + self.spare[0][0] <= at + 0.5):
                self.work(*self.spare.pop(0))
            turn += 1
            self.now = max(self.now, at)
            made.wait_recv()
            then()
            self.issue()
        while self.spare:
            self.work(*self.spare.pop(0))

    def finish(self):
        for made in self.copies:
            made.wait_send()


class Count:
    def __init__(self, n, then):
        self.n, self.then = n, then

    def __call__(self):
        self.n -= 1
        if self.n == 0:
            self.then()


def ring(net, n, me, axis, block, size, landed, far, urgency):
    reach = n // 2

    def step(way, s):
        part, share = (ALL, 1.0) if s < reach else far[way]
        if part is None:
            return
        ref = block(lax.rem(me - way * (s - 1) + n, n), part)
        to = lax.rem(me + way + n, n)
        net.send(ref, ref, {axis: to}, axis + ("+" if way == 1 else "-"), size * share, lambda: arrived(way, s), urgency)

    def arrived(way, s):
        if s < reach:
            step(way, s + 1)
        landed((n - way * s) % n)

    step(1, 1)
    step(-1, 1)


def ring_gather(net, n, me, axis, block, size, done, urgency=0):
    count = Count(n, done)
    ring(net, n, me, axis, block, size, lambda d: count(), {1: (0, 0.5), -1: (1, 0.5)}, urgency)


def kernel(
    tok,
    gate_left,
    gate_right,
    gate_values,
    gate_rows,
    gate_cols,
    up_left,
    up_right,
    up_values,
    up_rows,
    up_cols,
    grad_hidden,
    table,
    hidden,
    out_gate,
    out_up,
    t_all,
    t_perm,
    t_turn,
    left,
    right,
    shards,
    blocks,
    rank,
    pre,
    chain,
    up_stream,
    dpre,
    back,
    grads,
    came_up,
    came_down,
    leave_up,
    leave_down,
    mine,
    parcels,
    arrived_parcels,
    send_sems,
    recv_sems,
    local_sems,
):
    x, yl, z = lax.axis_index("x"), lax.axis_index("yl"), lax.axis_index("z")
    yh, c = lax.axis_index("yh"), lax.axis_index("c")
    other = 1 - yl

    def round_x(d):
        return lax.rem(x + d + NX, NX)

    def round_z(d):
        return lax.rem(z + d + NZ, NZ)

    pair, twin = {"yl": other}, {"c": 1 - c}
    across, beyond = {"yh": 1 - yh}, {"yh": 1 - yh, "yl": other}
    near = [{"x": round_x(d), "yl": yl if e == 0 else other} for d in range(NX) for e in range(NL)][1:]
    greeted = [twin, across, beyond, {"z": round_z(1)}, {"z": round_z(-1)}, *near]
    barrier = pltpu.get_barrier_semaphore()
    for who in greeted:
        pl.semaphore_signal(barrier, inc=1, device_id=who, device_id_type=pl.DeviceIdType.MESH)

    keeps = []

    def keep(src, dst):
        made = pltpu.make_async_copy(src, dst, local_sems.at[len(keeps)])
        made.start()
        keeps.append(made)

    def cols(ref, which):
        return ref.at[:, pl.ds(pl.multiple_of(which * HALF, BLK), HALF)]

    own_rows = pl.ds(pl.multiple_of(yl * BLK, BLK), BLK)
    other_rows = pl.ds(pl.multiple_of(other * BLK, BLK), BLK)
    keep(cols(gate_right, yl), right.at[x, yl, z, 0])
    keep(cols(up_right, yl), right.at[x, yl, z, 1])
    keep(tok, t_all.at[own_rows])
    keep(cols(grad_hidden, yl), up_stream.at[own_rows])
    own_left = pltpu.make_async_copy(gate_left, left.at[x, yl, z], local_sems.at[len(keeps)])

    @pl.when(yl == 0)
    def _():
        own_left.start()

    @pl.when(yl == 1)
    def _():
        pltpu.make_async_copy(up_left, left.at[x, yl, z], local_sems.at[len(keeps)]).start()

    keeps.append(own_left)
    shards[x, yl] = jnp.zeros((2, 32, 2 * BLK), BF16)
    shards[x, yl, 0, 0:KB] = gate_values[...]
    shards[x, yl, 1, 0:KB] = up_values[...]

    pl.semaphore_wait(barrier, len(greeted))
    net = Net(send_sems, recv_sems)

    def do_rank():
        total = jnp.zeros((2 * BLK, TILE), F32)
        for i in range(NX):
            total += dot(t_all[:, i * 1024 : (i + 1) * 1024], left[i].reshape(1024, TILE))
        slot = yl * 4 + yh * 2 + c
        rank[slot] = total.astype(BF16)

    def rank_slot(l, h, core):
        return rank.at[l * 4 + h * 2 + core]

    def share_rank():
        def on(l, h):
            ref = rank_slot(l, h, c)
            net.send(ref, ref, twin, "c", 0.131, rank_there)

        ref = rank_slot(yl, yh, c)
        net.send(ref, ref, pair, "y", 0.131, lambda: on(other, yh))
        net.send(ref, ref, beyond, "y", 0.0, lambda: on(other, 1 - yh))
        net.send(ref, ref, across, "y", 0.0, lambda: on(yl, 1 - yh))
        on(yl, yh)

    def gated(j):
        for h in range(2):
            for rows, mine_too in ((other_rows, False), (own_rows, True)):
                lanes = slice(h * BLK, (h + 1) * BLK)
                col = j * 2 + h
                gate = pre[0, rows, lanes] + chain[table[32 + yl * 14 + col], rows, :]
                up = pre[1, rows, lanes] + chain[28 + table[96 + yl * 14 + col], rows, :]
                coming = up_stream[rows, pl.ds(pl.multiple_of(col * BLK, BLK), BLK)].astype(F32)
                sigma = jax.nn.sigmoid(gate)
                silu = gate * sigma
                unit = (silu * up).astype(BF16)
                dpre[col, rows, :] = (coming * up * sigma * (1.0 + gate * (1.0 - sigma))).astype(BF16)
                dpre[14 + col, rows, :] = (coming * silu).astype(BF16)
                if mine_too:
                    hidden[:, pl.ds(pl.multiple_of(yl * HALF + col * BLK, BLK), BLK)] = unit
                else:
                    back[:, pl.ds(pl.multiple_of(col * BLK, BLK), BLK)] = unit

    def low_rank_and_gate(first, last):
        def do(j, _):
            at = pl.ds(pl.multiple_of(j * TILE, TILE), TILE)
            for g in range(2):
                total = jnp.zeros((2 * BLK, TILE), F32)
                for i in range(NX):
                    total += dot(rank[g * 4 + i], right[i, :, :, g, :, at].reshape(TILE, TILE))
                pre[g] = total
            gated(j)
            return 0

        lax.fori_loop(first, last, do, 0)

    def part_there(part):
        first, last = part[0] // TILE, part[1] // TILE
        for j in range(first, last, 2):
            end = min(j + 2, last)
            net.spare.append((0.8 * (end - j), lambda a=(j, end): low_rank_and_gate(*a)))

    part_ready = [Count(3, lambda p=p: part_there(p)) for p in PARTS]

    def all_ranks():
        for ready in part_ready:
            ready()

    rank_there = Count(7 - 3, all_ranks)

    def rank_ready():
        net.window.update({2: MIDDLE, 3: MIDDLE})
        net.work(1.0, do_rank)
        share_rank()

    left_parts = Count(2 + 1, rank_ready)

    def permute_tokens(first, last):
        new = lax.broadcasted_iota(jnp.int32, (BLK, BLK), 0)
        old = lax.broadcasted_iota(jnp.int32, (BLK, BLK), 1)

        def source(m):
            shard = ((m >> 1) & 3) * 16 + (m & 1) * 8 + (m >> 4)
            return shard * 2 + ((m >> 3) & 1)

        turn = (source(new) == old).astype(F32).astype(BF16)
        straight = (source(old) == new).astype(F32).astype(BF16)

        def do(i, _):
            for u in range(4):
                r = i * 4 + u
                part = t_all[:, pl.ds(pl.multiple_of(r * BLK, BLK), BLK)]
                t_perm[r] = dot(part, straight).astype(BF16)
                t_turn[r] = lax.dot_general(
                    turn, part, (((1,), (1,)), ((), ())), preferred_element_type=F32
                ).astype(BF16)
            return 0

        lax.fori_loop(first // 4, last // 4, do, 0)

    def sparse(g, rows_ref, first, last):
        def do(i, _):
            some = [i * 3 + u for u in range(3)]
            pieces = [dot(t_perm[rows_ref[k]], blocks[g * KB + k]) for k in some]
            for k, piece in zip(some, pieces):
                chain[g * 28 + k + 1] = piece + chain[g * 28 + table[g * 64 + k]]
            return 0

        lax.fori_loop(first // 3, last // 3, do, 0)
        if g == 1 and last == KB:
            all_ranks()

    def zero_chain():
        chain[0] = jnp.zeros((2 * BLK, BLK), F32)
        chain[28] = jnp.zeros((2 * BLK, BLK), F32)

    def all_sparse():
        net.spare.append((0.2, zero_chain))
        for g, rows_ref in ((0, gate_rows), (1, up_rows)):
            for first in range(0, KB, 9):
                net.spare.append((0.5, lambda a=(g, rows_ref, first, first + 9): sparse(*a)))

    sparse_ready = Count(2, all_sparse)

    def tokens_there():
        left_parts()
        for first in range(0, 32, 8):
            net.spare.append((0.4, lambda a=(first, first + 8): permute_tokens(*a)))
        sparse_ready()

    def spread_values():
        row = lax.broadcasted_iota(jnp.int32, (KB * 16, 512), 0)
        col = lax.broadcasted_iota(jnp.int32, (KB * 16, 512), 1)
        pick = col == (((row >> 3) & 1) * 256 + (row & 7) * 32 + (row >> 4))
        pick = pick.astype(F32).astype(BF16)
        for g in range(2):
            flat = shards[:, :, g].reshape(256, 2 * BLK)
            tall = jnp.concatenate([flat[:, :BLK], flat[:, BLK:]], axis=0)
            laid = dot(pick, tall).astype(BF16).reshape(KB, 16, BLK)
            blocks[g * KB : (g + 1) * KB, pl.ds(pl.multiple_of(z * 16, 16), 16), :] = laid

    def value_slice(i, half):
        some = {0: slice(0, KB), 1: slice(KB, 2 * KB)}.get(half if isinstance(half, int) else None, ALL)
        return blocks.at[some, pl.ds(pl.multiple_of(i * 16, 16), 16), :]

    def values_near():
        net.work(1.0, spread_values)
        ring_gather(net, NZ, z, "z", value_slice, 0.221, sparse_ready, VALUES)

    def gather(parts):
        counts = [[Count(2, lambda d=d, f=far: f(d)) for d in range(NX if x_first else NZ)] for x_first, _, _, far, _ in parts]

        def begin(half, way):
            far_way = {way: (ALL, 1.0), -way: (None, 0.0)}
            for (x_first, ref, size, _, urgency), count in zip(parts, counts):
                n, me, axis = (NX, x, "x") if x_first else (NZ, z, "z")
                ring(net, n, me, axis, lambda i, _, ref=ref: ref(i, half), size, lambda d, t=count: t[d](), far_way, urgency)
                count[0]()

        return (lambda: begin(yl, 1)), (lambda: begin(other, -1))

    def left_gather():
        parts = []
        for x_first, rows in ((True, slice(0, LEFT_A)), (False, slice(LEFT_A, 64))):
            everything = Count(NX if x_first else NZ, left_parts)
            size = (rows.stop - rows.start) * 0.131 / 128

            def near(i, h, x_first=x_first, rows=rows):
                return left.at[i, h, z, rows] if x_first else left.at[x, h, i, rows]

            def far(d, x_first=x_first, rows=rows, size=size, everything=everything):
                if x_first:
                    i = round_x(d)
                    ring_gather(net, NZ, z, "z", lambda k, h: left.at[i, h, k, rows], size, everything)
                else:
                    i = round_z(d)
                    ring_gather(net, NX, x, "x", lambda k, h: left.at[k, h, i, rows], size, everything)

            parts.append((x_first, near, size / 2, far, 0))
        return gather(parts)

    def right_gather():
        parts = []
        for p, (first, last) in enumerate(PARTS):
            x_first, span = p == 0, slice(first, last)
            everything = Count(NX if x_first else NZ, part_ready[p])
            size = (last - first) * 128e-6
            urgency = FAR if p < 2 else LATE

            def near(i, h, x_first=x_first, span=span):
                return right.at[i, h, z, :, :, span] if x_first else right.at[x, h, i, :, :, span]

            def far(d, x_first=x_first, span=span, size=size, everything=everything, urgency=urgency):
                if x_first:
                    i = round_x(d)
                    ring_gather(net, NZ, z, "z", lambda k, h: right.at[i, h, k, :, :, span], size, everything, urgency)
                else:
                    i = round_z(d)
                    ring_gather(net, NX, x, "x", lambda k, h: right.at[k, h, i, :, :, span], size, everything, urgency)

            parts.append((x_first, near, size / 2, far, NEAR if p < 2 else VALUES))
        return gather(parts)

    swap_left = net.copy(up_left, left.at[x, yl, z], pair)

    @pl.when(yl == 0)
    def _():
        swap_left.start()

    @pl.when(yl == 1)
    def _():
        net.copy(gate_left, left.at[x, yl, z], pair).start()

    for made in keeps:
        made.wait()
    left_own, left_other = left_gather()
    right_own, right_other = right_gather()
    net.track(swap_left, "y", 0.033, left_other)
    swapped_right = Count(2, right_other)
    net.send(cols(gate_right, other), right.at[x, yl, z, 0], pair, "y", 0.057, swapped_right)
    net.send(cols(up_right, other), right.at[x, yl, z, 1], pair, "y", 0.057, swapped_right)
    net.send(
        shards.at[x, yl],
        shards.at[x, yl],
        pair,
        "y",
        0.033,
        lambda: ring_gather(net, NX, x, "x", lambda i, h: shards.at[i, h], 0.066, values_near, 1),
    )
    mine_half = pl.ds(pl.multiple_of(c * 64, 64), 64)
    sent_half = pl.ds(pl.multiple_of(yl * BLK + c * 64, 64), 64)
    got_half = pl.ds(pl.multiple_of(other * BLK + c * 64, 64), 64)
    net.send(
        tok.at[mine_half],
        t_all.at[sent_half],
        pair,
        "y",
        0.524,
        lambda: net.send(t_all.at[got_half], t_all.at[got_half], twin, "c", 0.524, tokens_there),
    )
    net.send(cols(grad_hidden, other), up_stream.at[own_rows], pair, "y", 0.459, lambda: None)
    left_own()
    right_own()
    net.run()

    net.send(back, cols(hidden, yl), pair, "y", 0.459, lambda: None)

    def lot(i):
        return pl.ds(pl.multiple_of(i * 16, 16), 16)

    def to_owners(g):
        these = slice(g * KB, (g + 1) * KB)
        total = grads[these, lot(z), :] + came_up[3, these].astype(F32) + came_down[3, these].astype(F32)
        mine[g] = total.reshape(KB * 16, BLK)
        for s in range(8):
            for p in range(2):
                parcels[s, g, 0:KB, p * BLK : (p + 1) * BLK] = mine[g, pl.ds(p * 8 + s, KB, stride=16), :]
        for d in range(NX):
            for e in range(NL):
                if d == 0 and e == 0:
                    continue
                to_x, to_l = round_x(d), (yl if e == 0 else other)
                net.send(
                    parcels.at[to_x * 2 + to_l, g],
                    arrived_parcels.at[d * 2 + e, g],
                    {"x": to_x, "yl": to_l},
                    "owner",
                    0.033,
                    lambda: None,
                )

    def sum_round_z(g):
        begin, middle, end = g * KB, g * KB + 14, (g + 1) * KB
        home = Count(2, lambda: to_owners(g))

        def pass_on(way, j):
            came, leaves = (came_up, leave_up) if way == 1 else (came_down, leave_down)
            at = lot(round_z(way * (5 - j)))
            half, rest = (slice(begin, middle), slice(middle, end))[::way]
            these = half if j == 1 else slice(begin, end)
            if j == 1:
                leaves[0, half] = grads[half, at, :].astype(BF16)
            elif j == 2:
                leaves[1, half] = (grads[half, at, :] + came[0, half].astype(F32)).astype(BF16)
                leaves[1, rest] = grads[rest, at, :].astype(BF16)
            else:
                leaves[j - 1, these] = (grads[these, at, :] + came[j - 2, these].astype(F32)).astype(BF16)
            net.send(
                leaves.at[j - 1, these],
                came.at[j - 1, these],
                {"z": round_z(way)},
                "z+" if way == 1 else "z-",
                0.055 if j == 1 else 0.11,
                lambda: home() if j == 4 else pass_on(way, j + 1),
            )

        pass_on(1, 1)
        pass_on(-1, 1)

    for g, rows_ref, cols_ref in ((0, gate_rows, gate_cols), (1, up_rows, up_cols)):

        def gradient(i, _, g=g, rows_ref=rows_ref, cols_ref=cols_ref):
            for k in [i * 3 + u for u in range(3)]:
                col = cols_ref[k] - (yh * 2 + c) * 28 - yl * 14
                inside = (col >= 0) & (col < 14)
                term = dot(t_turn[rows_ref[k]], dpre[g * 14 + jnp.clip(col, 0, 13)])
                grads[g * KB + k] = jnp.where(inside, term, 0.0)
            return 0

        lax.fori_loop(0, KB // 3, gradient, 0)
        sum_round_z(g)
        net.now += 1.0
    net.run()
    total = parcels[x * 2 + yl]
    for i in range(1, 8):
        total = total + arrived_parcels[i]
    out_gate[...] = total[0, 0:KB]
    out_up[...] = total[1, 0:KB]
    net.finish()


def chains(gate_cols, up_cols, base):
    cols = jnp.stack([gate_cols, up_cols]) - base
    index = jnp.arange(64, dtype=jnp.int32)
    padded = jnp.pad(cols, ((0, 0), (0, 64 - KB)))
    asked = jnp.where(index < 32, padded, index - 32)
    limit = jnp.where(index < 32, index, KB)
    earlier = jnp.arange(KB, dtype=jnp.int32)
    hit = (cols[:, None, :] == asked[:, :, None]) & (earlier < limit[:, None])
    return jnp.max(jnp.where(hit, earlier + 1, 0), axis=2).reshape(128)


def on_device(*args):
    base = (lax.axis_index("yh") * 2 + lax.axis_index("c")) * 28
    table = chains(args[5], args[10], base)
    vmem, smem = pl.BlockSpec(memory_space=pltpu.VMEM), pl.BlockSpec(memory_space=pltpu.SMEM)
    specs = [vmem, vmem, vmem, vmem, smem, smem, vmem, vmem, vmem, smem, smem, vmem, smem]
    copies = 320
    return pl.pallas_call(
        kernel,
        out_shape=(
            jax.ShapeDtypeStruct((BLK, 2 * HALF), BF16),
            jax.ShapeDtypeStruct((KB, 2 * BLK), F32),
            jax.ShapeDtypeStruct((KB, 2 * BLK), F32),
        ),
        in_specs=specs,
        out_specs=(vmem, vmem, vmem),
        scratch_shapes=[
            pltpu.VMEM((2 * BLK, 4096), BF16),
            pltpu.VMEM((32, 2 * BLK, BLK), BF16),
            pltpu.VMEM((32, BLK, 2 * BLK), BF16),
            pltpu.VMEM((NX, NL, NZ, 64, TILE), BF16),
            pltpu.VMEM((NX, NL, NZ, 2, 16, HALF), BF16),
            pltpu.VMEM((NX, NL, 2, 32, 2 * BLK), BF16),
            pltpu.VMEM((2 * KB, BLK, BLK), BF16),
            pltpu.VMEM((8, 2 * BLK, TILE), BF16),
            pltpu.VMEM((2, 2 * BLK, TILE), F32),
            pltpu.VMEM((56, 2 * BLK, BLK), F32),
            pltpu.VMEM((2 * BLK, HALF), BF16),
            pltpu.VMEM((28, 2 * BLK, BLK), BF16),
            pltpu.VMEM((BLK, HALF), BF16),
            pltpu.VMEM((2 * KB, BLK, BLK), F32),
            pltpu.VMEM((4, 2 * KB, 16, BLK), BF16),
            pltpu.VMEM((4, 2 * KB, 16, BLK), BF16),
            pltpu.VMEM((4, 2 * KB, 16, BLK), BF16),
            pltpu.VMEM((4, 2 * KB, 16, BLK), BF16),
            pltpu.VMEM((2, KB * 16, BLK), F32),
            pltpu.VMEM((8, 2, 32, 2 * BLK), F32),
            pltpu.VMEM((8, 2, 32, 2 * BLK), F32),
            pltpu.SemaphoreType.DMA((copies,)),
            pltpu.SemaphoreType.DMA((copies,)),
            pltpu.SemaphoreType.DMA((8,)),
        ],
        compiler_params=pltpu.CompilerParams(
            collective_id=0, has_side_effects=True, vmem_limit_bytes=58 * 2**20
        ),
    )(*args, table)


def solution(mesh):
    finer = Mesh(mesh.devices.reshape(NX, NL, NZ, NH, NC), (*FSDP, *TP))
    return jax.shard_map(
        on_device,
        mesh=finer,
        in_specs=(
            P(FSDP, None),
            P(FSDP, TP),
            P(FSDP, TP),
            P(TP, FSDP),
            P(TP),
            P(TP),
            P(FSDP, TP),
            P(FSDP, TP),
            P(TP, FSDP),
            P(TP),
            P(TP),
            P(FSDP, TP),
        ),
        out_specs=(P(FSDP, TP), P(TP, FSDP), P(TP, FSDP)),
        check_vma=False,
    )
```

```python
import heapq

import jax
import jax.numpy as jnp
from jax import lax
from jax.experimental import pallas as pl
from jax.experimental.pallas import tpu as pltpu
from jax.sharding import Mesh
from jax.sharding import PartitionSpec as P

BLK = 128
NX, NL, NZ, NH, NC = 4, 2, 8, 2, 2
FSDP = ("x", "yl", "z")
TP = ("yh", "c")
KB = 27
HALF = 1792
TILE = 256
PARTS = ((0, 512), (512, 1280), (1280, 1792))
LEFT_A = 16
ALL = slice(None)
WIDE, MIDDLE, TIGHT = 50.0, 8.0, 3.0
NEAR, VALUES, FAR, LATE = 1, 1, 2, 3
F32, BF16 = jnp.float32, jnp.bfloat16


def dot(a, b):
    return jnp.dot(a, b, preferred_element_type=F32)


class Net:
    LATENCY = 3.0
    RATE = {"x+": 0.045, "x-": 0.045, "z+": 0.045, "z-": 0.045, "y": 0.045, "c": 0.2, "owner": 0.1}

    def __init__(self, send_sems, recv_sems):
        self.sems = (send_sems, recv_sems)
        self.now, self.free, self.heap, self.copies, self.spare = 0.0, {}, [], [], []
        self.waiting, self.asked = {}, 0
        self.window = {0: WIDE, 1: MIDDLE, 2: TIGHT, 3: TIGHT}

    def copy(self, src, dst, where):
        i = len(self.copies)
        made = pltpu.make_async_remote_copy(
            src_ref=src,
            dst_ref=dst,
            send_sem=self.sems[0].at[i],
            recv_sem=self.sems[1].at[i],
            device_id=where,
            device_id_type=pl.DeviceIdType.MESH,
        )
        return made

    def track(self, made, link, size, then):
        self.copies.append(made)
        begin = max(self.now, self.free.get(link, 0.0))
        self.free[link] = begin + size / self.RATE[link]
        heapq.heappush(self.heap, (self.free[link] + self.LATENCY, len(self.copies), made, then))

    def send(self, src, dst, where, link, size, then, urgency=0):
        self.asked += 1
        order = (urgency, self.asked)
        heapq.heappush(self.waiting.setdefault(link, []), (order, src, dst, where, size, then))
        self.issue()

    def issue(self):
        for link, queue in self.waiting.items():
            while queue and self.free.get(link, 0.0) < self.now + self.window[queue[0][0][0]]:
                _, src, dst, where, size, then = heapq.heappop(queue)
                made = self.copy(src, dst, where)
                made.start()
                self.track(made, link, size, then)

    def work(self, cost, do):
        do()
        self.now += cost
        self.issue()

    def run(self):
        turn = 0
        while self.heap:
            at, _, made, then = heapq.heappop(self.heap)
            if self.spare and (turn % 2 or self.now + self.spare[0][0] <= at + 0.5):
                self.work(*self.spare.pop(0))
            turn += 1
            self.now = max(self.now, at)
            made.wait_recv()
            then()
            self.issue()
        while self.spare:
            self.work(*self.spare.pop(0))

    def finish(self):
        for made in self.copies:
            made.wait_send()


class Count:
    def __init__(self, n, then):
        self.n, self.then = n, then

    def __call__(self):
        self.n -= 1
        if self.n == 0:
            self.then()


def ring(net, n, me, axis, block, size, landed, far, urgency):
    reach = n // 2

    def step(way, s):
        part, share = (ALL, 1.0) if s < reach else far[way]
        if part is None:
            return
        ref = block(lax.rem(me - way * (s - 1) + n, n), part)
        to = lax.rem(me + way + n, n)
        net.send(ref, ref, {axis: to}, axis + ("+" if way == 1 else "-"), size * share, lambda: arrived(way, s), urgency)

    def arrived(way, s):
        if s < reach:
            step(way, s + 1)
        landed((n - way * s) % n)

    step(1, 1)
    step(-1, 1)


def ring_gather(net, n, me, axis, block, size, done, urgency=0):
    count = Count(n, done)
    ring(net, n, me, axis, block, size, lambda d: count(), {1: (0, 0.5), -1: (1, 0.5)}, urgency)


def kernel(
    tok,
    gate_left,
    gate_right,
    gate_values,
    gate_rows,
    gate_cols,
    up_left,
    up_right,
    up_values,
    up_rows,
    up_cols,
    grad_hidden,
    table,
    hidden,
    out_gate,
    out_up,
    t_all,
    t_perm,
    t_turn,
    left,
    right,
    shards,
    blocks,
    rank,
    pre,
    chain,
    up_stream,
    dpre,
    back,
    grads,
    came_up,
    came_down,
    leave_up,
    leave_down,
    mine,
    parcels,
    arrived_parcels,
    send_sems,
    recv_sems,
    local_sems,
):
    x, yl, z = lax.axis_index("x"), lax.axis_index("yl"), lax.axis_index("z")
    yh, c = lax.axis_index("yh"), lax.axis_index("c")
    other = 1 - yl

    def round_x(d):
        return lax.rem(x + d + NX, NX)

    def round_z(d):
        return lax.rem(z + d + NZ, NZ)

    pair, twin = {"yl": other}, {"c": 1 - c}
    across, beyond = {"yh": 1 - yh}, {"yh": 1 - yh, "yl": other}
    near = [{"x": round_x(d), "yl": yl if e == 0 else other} for d in range(NX) for e in range(NL)][1:]
    greeted = [twin, across, beyond, {"z": round_z(1)}, {"z": round_z(-1)}, *near]
    barrier = pltpu.get_barrier_semaphore()
    for who in greeted:
        pl.semaphore_signal(barrier, inc=1, device_id=who, device_id_type=pl.DeviceIdType.MESH)

    keeps = []

    def keep(src, dst):
        made = pltpu.make_async_copy(src, dst, local_sems.at[len(keeps)])
        made.start()
        keeps.append(made)

    def cols(ref, which):
        return ref.at[:, pl.ds(pl.multiple_of(which * HALF, BLK), HALF)]

    own_rows = pl.ds(pl.multiple_of(yl * BLK, BLK), BLK)
    other_rows = pl.ds(pl.multiple_of(other * BLK, BLK), BLK)
    keep(cols(gate_right, yl), right.at[x, yl, z, 0])
    keep(cols(up_right, yl), right.at[x, yl, z, 1])
    keep(tok, t_all.at[own_rows])
    keep(cols(grad_hidden, yl), up_stream.at[own_rows])
    own_left = pltpu.make_async_copy(gate_left, left.at[x, yl, z], local_sems.at[len(keeps)])

    @pl.when(yl == 0)
    def _():
        own_left.start()

    @pl.when(yl == 1)
    def _():
        pltpu.make_async_copy(up_left, left.at[x, yl, z], local_sems.at[len(keeps)]).start()

    keeps.append(own_left)
    shards[x, yl] = jnp.zeros((2, 32, 2 * BLK), BF16)
    shards[x, yl, 0, 0:KB] = gate_values[...]
    shards[x, yl, 1, 0:KB] = up_values[...]

    pl.semaphore_wait(barrier, len(greeted))
    net = Net(send_sems, recv_sems)

    def do_rank():
        total = jnp.zeros((2 * BLK, TILE), F32)
        for i in range(NX):
            total += dot(t_all[:, i * 1024 : (i + 1) * 1024], left[i].reshape(1024, TILE))
        slot = yl * 4 + yh * 2 + c
        rank[slot] = total.astype(BF16)

    def rank_slot(l, h, core):
        return rank.at[l * 4 + h * 2 + core]

    def share_rank():
        def on(l, h):
            ref = rank_slot(l, h, c)
            net.send(ref, ref, twin, "c", 0.131, rank_there)

        ref = rank_slot(yl, yh, c)
        net.send(ref, ref, pair, "y", 0.131, lambda: on(other, yh))
        net.send(ref, ref, beyond, "y", 0.0, lambda: on(other, 1 - yh))
        net.send(ref, ref, across, "y", 0.0, lambda: on(yl, 1 - yh))
        on(yl, yh)

    def gated(j):
        for h in range(2):
            for rows, mine_too in ((other_rows, False), (own_rows, True)):
                lanes = slice(h * BLK, (h + 1) * BLK)
                col = j * 2 + h
                gate = pre[0, rows, lanes] + chain[table[32 + yl * 14 + col], rows, :]
                up = pre[1, rows, lanes] + chain[28 + table[96 + yl * 14 + col], rows, :]
                coming = up_stream[rows, pl.ds(pl.multiple_of(col * BLK, BLK), BLK)].astype(F32)
                sigma = jax.nn.sigmoid(gate)
                silu = gate * sigma
                unit = (silu * up).astype(BF16)
                dpre[col, rows, :] = (coming * up * sigma * (1.0 + gate * (1.0 - sigma))).astype(BF16)
                dpre[14 + col, rows, :] = (coming * silu).astype(BF16)
                if mine_too:
                    hidden[:, pl.ds(pl.multiple_of(yl * HALF + col * BLK, BLK), BLK)] = unit
                else:
                    back[:, pl.ds(pl.multiple_of(col * BLK, BLK), BLK)] = unit

    def low_rank_and_gate(first, last):
        def do(j, _):
            at = pl.ds(pl.multiple_of(j * TILE, TILE), TILE)
            for g in range(2):
                total = jnp.zeros((2 * BLK, TILE), F32)
                for i in range(NX):
                    total += dot(rank[g * 4 + i], right[i, :, :, g, :, at].reshape(TILE, TILE))
                pre[g] = total
            gated(j)
            return 0

        lax.fori_loop(first, last, do, 0)

    def part_there(part):
        first, last = part[0] // TILE, part[1] // TILE
        for j in range(first, last, 2):
            end = min(j + 2, last)
            net.spare.append((0.8 * (end - j), lambda a=(j, end): low_rank_and_gate(*a)))

    part_ready = [Count(3, lambda p=p: part_there(p)) for p in PARTS]

    def all_ranks():
        for ready in part_ready:
            ready()

    rank_there = Count(7 - 3, all_ranks)

    def rank_ready():
        net.window.update({2: MIDDLE, 3: MIDDLE})
        net.work(1.0, do_rank)
        share_rank()

    left_parts = Count(2 + 1, rank_ready)

    def permute_tokens(first, last):
        new = lax.broadcasted_iota(jnp.int32, (BLK, BLK), 0)
        old = lax.broadcasted_iota(jnp.int32, (BLK, BLK), 1)

        def source(m):
            shard = ((m >> 1) & 3) * 16 + (m & 1) * 8 + (m >> 4)
            return shard * 2 + ((m >> 3) & 1)

        turn = (source(new) == old).astype(F32).astype(BF16)
        straight = (source(old) == new).astype(F32).astype(BF16)

        def do(i, _):
            for u in range(4):
                r = i * 4 + u
                part = t_all[:, pl.ds(pl.multiple_of(r * BLK, BLK), BLK)]
                t_perm[r] = dot(part, straight).astype(BF16)
                t_turn[r] = lax.dot_general(
                    turn, part, (((1,), (1,)), ((), ())), preferred_element_type=F32
                ).astype(BF16)
            return 0

        lax.fori_loop(first // 4, last // 4, do, 0)

    def sparse(g, rows_ref, first, last):
        def do(i, _):
            some = [i * 3 + u for u in range(3)]
            pieces = [dot(t_perm[rows_ref[k]], blocks[g * KB + k]) for k in some]
            for k, piece in zip(some, pieces):
                chain[g * 28 + k + 1] = piece + chain[g * 28 + table[g * 64 + k]]
            return 0

        lax.fori_loop(first // 3, last // 3, do, 0)
        if g == 1 and last == KB:
            all_ranks()

    def zero_chain():
        chain[0] = jnp.zeros((2 * BLK, BLK), F32)
        chain[28] = jnp.zeros((2 * BLK, BLK), F32)

    def all_sparse():
        net.spare.append((0.2, zero_chain))
        for g, rows_ref in ((0, gate_rows), (1, up_rows)):
            for first in range(0, KB, 9):
                net.spare.append((0.5, lambda a=(g, rows_ref, first, first + 9): sparse(*a)))

    sparse_ready = Count(2, all_sparse)

    def tokens_there():
        left_parts()
        for first in range(0, 32, 8):
            net.spare.append((0.4, lambda a=(first, first + 8): permute_tokens(*a)))
        sparse_ready()

    def spread_values():
        row = lax.broadcasted_iota(jnp.int32, (KB * 16, 512), 0)
        col = lax.broadcasted_iota(jnp.int32, (KB * 16, 512), 1)
        pick = col == (((row >> 3) & 1) * 256 + (row & 7) * 32 + (row >> 4))
        pick = pick.astype(F32).astype(BF16)
        for g in range(2):
            flat = shards[:, :, g].reshape(256, 2 * BLK)
            tall = jnp.concatenate([flat[:, :BLK], flat[:, BLK:]], axis=0)
            laid = dot(pick, tall).astype(BF16).reshape(KB, 16, BLK)
            blocks[g * KB : (g + 1) * KB, pl.ds(pl.multiple_of(z * 16, 16), 16), :] = laid

    def value_slice(i, half):
        some = {0: slice(0, KB), 1: slice(KB, 2 * KB)}.get(half if isinstance(half, int) else None, ALL)
        return blocks.at[some, pl.ds(pl.multiple_of(i * 16, 16), 16), :]

    def values_near():
        net.work(1.0, spread_values)
        ring_gather(net, NZ, z, "z", value_slice, 0.221, sparse_ready, VALUES)

    def gather(parts):
        counts = [[Count(2, lambda d=d, f=far: f(d)) for d in range(NX if x_first else NZ)] for x_first, _, _, far, _ in parts]

        def begin(half, way):
            far_way = {way: (ALL, 1.0), -way: (None, 0.0)}
            for (x_first, ref, size, _, urgency), count in zip(parts, counts):
                n, me, axis = (NX, x, "x") if x_first else (NZ, z, "z")
                ring(net, n, me, axis, lambda i, _, ref=ref: ref(i, half), size, lambda d, t=count: t[d](), far_way, urgency)
                count[0]()

        return (lambda: begin(yl, 1)), (lambda: begin(other, -1))

    def left_gather():
        parts = []
        for x_first, rows in ((True, slice(0, LEFT_A)), (False, slice(LEFT_A, 64))):
            everything = Count(NX if x_first else NZ, left_parts)
            size = (rows.stop - rows.start) * 0.131 / 128

            def near(i, h, x_first=x_first, rows=rows):
                return left.at[i, h, z, rows] if x_first else left.at[x, h, i, rows]

            def far(d, x_first=x_first, rows=rows, size=size, everything=everything):
                if x_first:
                    i = round_x(d)
                    ring_gather(net, NZ, z, "z", lambda k, h: left.at[i, h, k, rows], size, everything)
                else:
                    i = round_z(d)
                    ring_gather(net, NX, x, "x", lambda k, h: left.at[k, h, i, rows], size, everything)

            parts.append((x_first, near, size / 2, far, 0))
        return gather(parts)

    def right_gather():
        parts = []
        for p, (first, last) in enumerate(PARTS):
            x_first, span = p == 0, slice(first, last)
            everything = Count(NX if x_first else NZ, part_ready[p])
            size = (last - first) * 128e-6
            urgency = FAR if p < 2 else LATE

            def near(i, h, x_first=x_first, span=span):
                return right.at[i, h, z, :, :, span] if x_first else right.at[x, h, i, :, :, span]

            def far(d, x_first=x_first, span=span, size=size, everything=everything, urgency=urgency):
                if x_first:
                    i = round_x(d)
                    ring_gather(net, NZ, z, "z", lambda k, h: right.at[i, h, k, :, :, span], size, everything, urgency)
                else:
                    i = round_z(d)
                    ring_gather(net, NX, x, "x", lambda k, h: right.at[k, h, i, :, :, span], size, everything, urgency)

            parts.append((x_first, near, size / 2, far, NEAR if p < 2 else VALUES))
        return gather(parts)

    swap_left = net.copy(up_left, left.at[x, yl, z], pair)

    @pl.when(yl == 0)
    def _():
        swap_left.start()

    @pl.when(yl == 1)
    def _():
        net.copy(gate_left, left.at[x, yl, z], pair).start()

    at_first = (keeps[0], keeps[1], keeps[4])
    for made in at_first:
        made.wait()
    left_own, left_other = left_gather()
    right_own, right_other = right_gather()
    net.track(swap_left, "y", 0.033, left_other)
    swapped_right = Count(2, right_other)
    net.send(cols(gate_right, other), right.at[x, yl, z, 0], pair, "y", 0.057, swapped_right)
    net.send(cols(up_right, other), right.at[x, yl, z, 1], pair, "y", 0.057, swapped_right)
    net.send(
        shards.at[x, yl],
        shards.at[x, yl],
        pair,
        "y",
        0.033,
        lambda: ring_gather(net, NX, x, "x", lambda i, h: shards.at[i, h], 0.066, values_near, 1),
    )
    mine_half = pl.ds(pl.multiple_of(c * 64, 64), 64)
    sent_half = pl.ds(pl.multiple_of(yl * BLK + c * 64, 64), 64)
    got_half = pl.ds(pl.multiple_of(other * BLK + c * 64, 64), 64)
    net.send(
        tok.at[mine_half],
        t_all.at[sent_half],
        pair,
        "y",
        0.524,
        lambda: net.send(t_all.at[got_half], t_all.at[got_half], twin, "c", 0.524, tokens_there),
    )
    net.send(cols(grad_hidden, other), up_stream.at[own_rows], pair, "y", 0.459, lambda: None)
    left_own()
    right_own()
    for made in keeps[2:4]:
        made.wait()
    net.run()

    net.send(back, cols(hidden, yl), pair, "y", 0.459, lambda: None)

    def lot(i):
        return pl.ds(pl.multiple_of(i * 16, 16), 16)

    def to_owners(g):
        these = slice(g * KB, (g + 1) * KB)
        total = grads[these, lot(z), :] + came_up[3, these].astype(F32) + came_down[3, these].astype(F32)
        mine[g] = total.reshape(KB * 16, BLK)
        for s in range(8):
            for p in range(2):
                parcels[s, g, 0:KB, p * BLK : (p + 1) * BLK] = mine[g, pl.ds(p * 8 + s, KB, stride=16), :]
        for d in range(NX):
            for e in range(NL):
                if d == 0 and e == 0:
                    continue
                to_x, to_l = round_x(d), (yl if e == 0 else other)
                net.send(
                    parcels.at[to_x * 2 + to_l, g],
                    arrived_parcels.at[d * 2 + e, g],
                    {"x": to_x, "yl": to_l},
                    "owner",
                    0.033,
                    lambda: None,
                )

    def sum_round_z(g):
        begin, middle, end = g * KB, g * KB + 14, (g + 1) * KB
        home = Count(2, lambda: to_owners(g))

        def pass_on(way, j):
            came, leaves = (came_up, leave_up) if way == 1 else (came_down, leave_down)
            at = lot(round_z(way * (5 - j)))
            half, rest = (slice(begin, middle), slice(middle, end))[::way]
            these = half if j == 1 else slice(begin, end)
            if j == 1:
                leaves[0, half] = grads[half, at, :].astype(BF16)
            elif j == 2:
                leaves[1, half] = (grads[half, at, :] + came[0, half].astype(F32)).astype(BF16)
                leaves[1, rest] = grads[rest, at, :].astype(BF16)
            else:
                leaves[j - 1, these] = (grads[these, at, :] + came[j - 2, these].astype(F32)).astype(BF16)
            net.send(
                leaves.at[j - 1, these],
                came.at[j - 1, these],
                {"z": round_z(way)},
                "z+" if way == 1 else "z-",
                0.055 if j == 1 else 0.11,
                lambda: home() if j == 4 else pass_on(way, j + 1),
            )

        pass_on(1, 1)
        pass_on(-1, 1)

    for g, rows_ref, cols_ref in ((0, gate_rows, gate_cols), (1, up_rows, up_cols)):

        def gradient(i, _, g=g, rows_ref=rows_ref, cols_ref=cols_ref):
            for k in [i * 3 + u for u in range(3)]:
                col = cols_ref[k] - (yh * 2 + c) * 28 - yl * 14
                inside = (col >= 0) & (col < 14)
                term = dot(t_turn[rows_ref[k]], dpre[g * 14 + jnp.clip(col, 0, 13)])
                grads[g * KB + k] = jnp.where(inside, term, 0.0)
            return 0

        lax.fori_loop(0, KB // 3, gradient, 0)
        sum_round_z(g)
        net.now += 1.0
    net.run()
    total = parcels[x * 2 + yl]
    for i in range(1, 8):
        total = total + arrived_parcels[i]
    out_gate[...] = total[0, 0:KB]
    out_up[...] = total[1, 0:KB]
    net.finish()


def chains(gate_cols, up_cols, base):
    cols = jnp.stack([gate_cols, up_cols]) - base
    index = jnp.arange(64, dtype=jnp.int32)
    padded = jnp.pad(cols, ((0, 0), (0, 64 - KB)))
    asked = jnp.where(index < 32, padded, index - 32)
    limit = jnp.where(index < 32, index, KB)
    earlier = jnp.arange(KB, dtype=jnp.int32)
    hit = (cols[:, None, :] == asked[:, :, None]) & (earlier < limit[:, None])
    return jnp.max(jnp.where(hit, earlier + 1, 0), axis=2).reshape(128)


def on_device(*args):
    base = (lax.axis_index("yh") * 2 + lax.axis_index("c")) * 28
    table = chains(args[5], args[10], base)
    vmem, smem = pl.BlockSpec(memory_space=pltpu.VMEM), pl.BlockSpec(memory_space=pltpu.SMEM)
    hbm = pl.BlockSpec(memory_space=pl.ANY)
    specs = [hbm, hbm, hbm, vmem, smem, smem, hbm, hbm, vmem, smem, smem, hbm, smem]
    copies = 320
    return pl.pallas_call(
        kernel,
        out_shape=(
            jax.ShapeDtypeStruct((BLK, 2 * HALF), BF16),
            jax.ShapeDtypeStruct((KB, 2 * BLK), F32),
            jax.ShapeDtypeStruct((KB, 2 * BLK), F32),
        ),
        in_specs=specs,
        out_specs=(vmem, vmem, vmem),
        scratch_shapes=[
            pltpu.VMEM((2 * BLK, 4096), BF16),
            pltpu.VMEM((32, 2 * BLK, BLK), BF16),
            pltpu.VMEM((32, BLK, 2 * BLK), BF16),
            pltpu.VMEM((NX, NL, NZ, 64, TILE), BF16),
            pltpu.VMEM((NX, NL, NZ, 2, 16, HALF), BF16),
            pltpu.VMEM((NX, NL, 2, 32, 2 * BLK), BF16),
            pltpu.VMEM((2 * KB, BLK, BLK), BF16),
            pltpu.VMEM((8, 2 * BLK, TILE), BF16),
            pltpu.VMEM((2, 2 * BLK, TILE), F32),
            pltpu.VMEM((56, 2 * BLK, BLK), F32),
            pltpu.VMEM((2 * BLK, HALF), BF16),
            pltpu.VMEM((28, 2 * BLK, BLK), BF16),
            pltpu.VMEM((BLK, HALF), BF16),
            pltpu.VMEM((2 * KB, BLK, BLK), F32),
            pltpu.VMEM((4, 2 * KB, 16, BLK), BF16),
            pltpu.VMEM((4, 2 * KB, 16, BLK), BF16),
            pltpu.VMEM((4, 2 * KB, 16, BLK), BF16),
            pltpu.VMEM((4, 2 * KB, 16, BLK), BF16),
            pltpu.VMEM((2, KB * 16, BLK), F32),
            pltpu.VMEM((8, 2, 32, 2 * BLK), F32),
            pltpu.VMEM((8, 2, 32, 2 * BLK), F32),
            pltpu.SemaphoreType.DMA((copies,)),
            pltpu.SemaphoreType.DMA((copies,)),
            pltpu.SemaphoreType.DMA((8,)),
        ],
        compiler_params=pltpu.CompilerParams(
            collective_id=0, has_side_effects=True, vmem_limit_bytes=58 * 2**20
        ),
    )(*args, table)


def solution(mesh):
    finer = Mesh(mesh.devices.reshape(NX, NL, NZ, NH, NC), (*FSDP, *TP))
    return jax.shard_map(
        on_device,
        mesh=finer,
        in_specs=(
            P(FSDP, None),
            P(FSDP, TP),
            P(FSDP, TP),
            P(TP, FSDP),
            P(TP),
            P(TP),
            P(FSDP, TP),
            P(FSDP, TP),
            P(TP, FSDP),
            P(TP),
            P(TP),
            P(FSDP, TP),
        ),
        out_specs=(P(FSDP, TP), P(TP, FSDP), P(TP, FSDP)),
        check_vma=False,
    )
```

```python
import heapq

import jax
import jax.numpy as jnp
from jax import lax
from jax.experimental import pallas as pl
from jax.experimental.pallas import tpu as pltpu
from jax.sharding import Mesh
from jax.sharding import PartitionSpec as P

BLK = 128
NX, NL, NZ, NH, NC = 4, 2, 8, 2, 2
FSDP = ("x", "yl", "z")
TP = ("yh", "c")
KB = 27
HALF = 1792
TILE = 256
PARTS = ((0, 512), (512, 1280), (1280, 1792))
LEFT_A = 16
ALL = slice(None)
WIDE, MIDDLE, TIGHT = 50.0, 8.0, 3.0
NEAR, VALUES, FAR, LATE = 1, 1, 2, 3
F32, BF16 = jnp.float32, jnp.bfloat16


def dot(a, b):
    return jnp.dot(a, b, preferred_element_type=F32)


class Net:
    LATENCY = 3.0
    RATE = {"x+": 0.045, "x-": 0.045, "z+": 0.045, "z-": 0.045, "y": 0.045, "c": 0.2, "owner": 0.1}

    def __init__(self, send_sems, recv_sems):
        self.sems = (send_sems, recv_sems)
        self.now, self.free, self.heap, self.copies, self.spare = 0.0, {}, [], [], []
        self.waiting, self.asked = {}, 0
        self.window = {0: WIDE, 1: MIDDLE, 2: TIGHT, 3: TIGHT}

    def copy(self, src, dst, where):
        i = len(self.copies)
        made = pltpu.make_async_remote_copy(
            src_ref=src,
            dst_ref=dst,
            send_sem=self.sems[0].at[i],
            recv_sem=self.sems[1].at[i],
            device_id=where,
            device_id_type=pl.DeviceIdType.MESH,
        )
        return made

    def track(self, made, link, size, then):
        self.copies.append(made)
        begin = max(self.now, self.free.get(link, 0.0))
        self.free[link] = begin + size / self.RATE[link]
        heapq.heappush(self.heap, (self.free[link] + self.LATENCY, len(self.copies), made, then))

    def send(self, src, dst, where, link, size, then, urgency=0):
        self.asked += 1
        order = (urgency, self.asked)
        heapq.heappush(self.waiting.setdefault(link, []), (order, src, dst, where, size, then))
        self.issue()

    def issue(self):
        for link, queue in self.waiting.items():
            while queue and self.free.get(link, 0.0) < self.now + self.window[queue[0][0][0]]:
                _, src, dst, where, size, then = heapq.heappop(queue)
                made = self.copy(src, dst, where)
                made.start()
                self.track(made, link, size, then)

    def work(self, cost, do):
        do()
        self.now += cost
        self.issue()

    def run(self):
        turn = 0
        while self.heap:
            at, _, made, then = heapq.heappop(self.heap)
            if self.spare and (turn % 2 or self.now + self.spare[0][0] <= at + 0.5):
                self.work(*self.spare.pop(0))
            turn += 1
            self.now = max(self.now, at)
            made.wait_recv()
            then()
            self.issue()
        while self.spare:
            self.work(*self.spare.pop(0))

    def finish(self):
        for made in self.copies:
            made.wait_send()


class Count:
    def __init__(self, n, then):
        self.n, self.then = n, then

    def __call__(self):
        self.n -= 1
        if self.n == 0:
            self.then()


def ring(net, n, me, axis, block, size, landed, far, urgency):
    reach = n // 2

    def step(way, s):
        part, share = (ALL, 1.0) if s < reach else far[way]
        if part is None:
            return
        ref = block(lax.rem(me - way * (s - 1) + n, n), part)
        to = lax.rem(me + way + n, n)
        net.send(ref, ref, {axis: to}, axis + ("+" if way == 1 else "-"), size * share, lambda: arrived(way, s), urgency)

    def arrived(way, s):
        if s < reach:
            step(way, s + 1)
        landed((n - way * s) % n)

    step(1, 1)
    step(-1, 1)


def ring_gather(net, n, me, axis, block, size, done, urgency=0):
    count = Count(n, done)
    ring(net, n, me, axis, block, size, lambda d: count(), {1: (0, 0.5), -1: (1, 0.5)}, urgency)


def kernel(
    tok,
    gate_left,
    gate_right,
    gate_values,
    gate_rows,
    gate_cols,
    up_left,
    up_right,
    up_values,
    up_rows,
    up_cols,
    grad_hidden,
    table,
    hidden,
    out_gate,
    out_up,
    t_all,
    t_perm,
    t_turn,
    left,
    right,
    shards,
    blocks,
    rank,
    pre,
    chain,
    up_stream,
    dpre,
    back,
    grads,
    came_up,
    came_down,
    leave_up,
    leave_down,
    mine,
    parcels,
    arrived_parcels,
    send_sems,
    recv_sems,
    local_sems,
):
    x, yl, z = lax.axis_index("x"), lax.axis_index("yl"), lax.axis_index("z")
    yh, c = lax.axis_index("yh"), lax.axis_index("c")
    other = 1 - yl

    def round_x(d):
        return lax.rem(x + d + NX, NX)

    def round_z(d):
        return lax.rem(z + d + NZ, NZ)

    pair, twin = {"yl": other}, {"c": 1 - c}
    across, beyond = {"yh": 1 - yh}, {"yh": 1 - yh, "yl": other}
    near = [{"x": round_x(d), "yl": yl if e == 0 else other} for d in range(NX) for e in range(NL)][1:]
    greeted = [twin, across, beyond, {"z": round_z(1)}, {"z": round_z(-1)}, *near]
    barrier = pltpu.get_barrier_semaphore()
    for who in greeted:
        pl.semaphore_signal(barrier, inc=1, device_id=who, device_id_type=pl.DeviceIdType.MESH)

    keeps = []

    def keep(src, dst):
        made = pltpu.make_async_copy(src, dst, local_sems.at[len(keeps)])
        made.start()
        keeps.append(made)

    def cols(ref, which):
        return ref.at[:, pl.ds(pl.multiple_of(which * HALF, BLK), HALF)]

    own_rows = pl.ds(pl.multiple_of(yl * BLK, BLK), BLK)
    other_rows = pl.ds(pl.multiple_of(other * BLK, BLK), BLK)
    keep(cols(gate_right, yl), right.at[x, yl, z, 0])
    keep(cols(up_right, yl), right.at[x, yl, z, 1])
    keep(tok, t_all.at[own_rows])
    keep(cols(grad_hidden, yl), up_stream.at[own_rows])
    own_left = pltpu.make_async_copy(gate_left, left.at[x, yl, z], local_sems.at[len(keeps)])

    @pl.when(yl == 0)
    def _():
        own_left.start()

    @pl.when(yl == 1)
    def _():
        pltpu.make_async_copy(up_left, left.at[x, yl, z], local_sems.at[len(keeps)]).start()

    keeps.append(own_left)
    shards[x, yl] = jnp.zeros((2, 32, 2 * BLK), BF16)
    shards[x, yl, 0, 0:KB] = gate_values[...]
    shards[x, yl, 1, 0:KB] = up_values[...]

    pl.semaphore_wait(barrier, len(greeted))
    net = Net(send_sems, recv_sems)

    def do_rank():
        total = jnp.zeros((2 * BLK, TILE), F32)
        for i in range(NX):
            total += dot(t_all[:, i * 1024 : (i + 1) * 1024], left[i].reshape(1024, TILE))
        slot = yl * 4 + yh * 2 + c
        rank[slot] = total.astype(BF16)

    def rank_slot(l, h, core):
        return rank.at[l * 4 + h * 2 + core]

    def share_rank():
        def on(l, h):
            ref = rank_slot(l, h, c)
            net.send(ref, ref, twin, "c", 0.131, rank_there)

        ref = rank_slot(yl, yh, c)
        net.send(ref, ref, pair, "y", 0.131, lambda: on(other, yh))
        net.send(ref, ref, beyond, "y", 0.0, lambda: on(other, 1 - yh))
        net.send(ref, ref, across, "y", 0.0, lambda: on(yl, 1 - yh))
        on(yl, yh)

    def gated(j):
        for h in range(2):
            for rows, mine_too in ((other_rows, False), (own_rows, True)):
                lanes = slice(h * BLK, (h + 1) * BLK)
                col = j * 2 + h
                gate = pre[0, rows, lanes] + chain[table[32 + yl * 14 + col], rows, :]
                up = pre[1, rows, lanes] + chain[28 + table[96 + yl * 14 + col], rows, :]
                coming = up_stream[rows, pl.ds(pl.multiple_of(col * BLK, BLK), BLK)].astype(F32)
                sigma = jax.nn.sigmoid(gate)
                silu = gate * sigma
                unit = (silu * up).astype(BF16)
                dpre[col, rows, :] = (coming * up * sigma * (1.0 + gate * (1.0 - sigma))).astype(BF16)
                dpre[14 + col, rows, :] = (coming * silu).astype(BF16)
                if mine_too:
                    hidden[:, pl.ds(pl.multiple_of(yl * HALF + col * BLK, BLK), BLK)] = unit
                else:
                    back[:, pl.ds(pl.multiple_of(col * BLK, BLK), BLK)] = unit

    def low_rank_and_gate(first, last):
        def do(j, _):
            at = pl.ds(pl.multiple_of(j * TILE, TILE), TILE)
            for g in range(2):
                total = jnp.zeros((2 * BLK, TILE), F32)
                for i in range(NX):
                    total += dot(rank[g * 4 + i], right[i, :, :, g, :, at].reshape(TILE, TILE))
                pre[g] = total
            gated(j)
            return 0

        lax.fori_loop(first, last, do, 0)

    def part_there(part):
        first, last = part[0] // TILE, part[1] // TILE
        for j in range(first, last, 2):
            end = min(j + 2, last)
            net.spare.append((0.8 * (end - j), lambda a=(j, end): low_rank_and_gate(*a)))

    part_ready = [Count(3, lambda p=p: part_there(p)) for p in PARTS]

    def all_ranks():
        for ready in part_ready:
            ready()

    rank_there = Count(7 - 3, all_ranks)

    def rank_ready():
        net.window.update({2: MIDDLE, 3: MIDDLE})
        net.work(1.0, do_rank)
        share_rank()

    left_parts = Count(2 + 1, rank_ready)

    def permute_tokens(first, last):
        new = lax.broadcasted_iota(jnp.int32, (BLK, BLK), 0)
        old = lax.broadcasted_iota(jnp.int32, (BLK, BLK), 1)

        def source(m):
            shard = ((m >> 1) & 3) * 16 + (m & 1) * 8 + (m >> 4)
            return shard * 2 + ((m >> 3) & 1)

        turn = (source(new) == old).astype(F32).astype(BF16)
        straight = (source(old) == new).astype(F32).astype(BF16)

        def do(i, _):
            for u in range(4):
                r = i * 4 + u
                part = t_all[:, pl.ds(pl.multiple_of(r * BLK, BLK), BLK)]
                t_perm[r] = dot(part, straight).astype(BF16)
                t_turn[r] = lax.dot_general(
                    turn, part, (((1,), (1,)), ((), ())), preferred_element_type=F32
                ).astype(BF16)
            return 0

        lax.fori_loop(first // 4, last // 4, do, 0)

    def sparse(g, rows_ref, first, last):
        def do(i, _):
            some = [i * 3 + u for u in range(3)]
            pieces = [dot(t_perm[rows_ref[k]], blocks[g * KB + k]) for k in some]
            for k, piece in zip(some, pieces):
                chain[g * 28 + k + 1] = piece + chain[g * 28 + table[g * 64 + k]]
            return 0

        lax.fori_loop(first // 3, last // 3, do, 0)
        if g == 1 and last == KB:
            all_ranks()

    def zero_chain():
        chain[0] = jnp.zeros((2 * BLK, BLK), F32)
        chain[28] = jnp.zeros((2 * BLK, BLK), F32)

    def all_sparse():
        net.spare.append((0.2, zero_chain))
        for g, rows_ref in ((0, gate_rows), (1, up_rows)):
            for first in range(0, KB, 9):
                net.spare.append((0.5, lambda a=(g, rows_ref, first, first + 9): sparse(*a)))

    sparse_ready = Count(2, all_sparse)

    def tokens_there():
        left_parts()
        for first in range(0, 32, 8):
            net.spare.append((0.4, lambda a=(first, first + 8): permute_tokens(*a)))
        sparse_ready()

    def spread_values():
        row = lax.broadcasted_iota(jnp.int32, (KB * 16, 512), 0)
        col = lax.broadcasted_iota(jnp.int32, (KB * 16, 512), 1)
        pick = col == (((row >> 3) & 1) * 256 + (row & 7) * 32 + (row >> 4))
        pick = pick.astype(F32).astype(BF16)
        for g in range(2):
            flat = shards[:, :, g].reshape(256, 2 * BLK)
            tall = jnp.concatenate([flat[:, :BLK], flat[:, BLK:]], axis=0)
            laid = dot(pick, tall).astype(BF16).reshape(KB, 16, BLK)
            blocks[g * KB : (g + 1) * KB, pl.ds(pl.multiple_of(z * 16, 16), 16), :] = laid

    def value_slice(i, half):
        some = {0: slice(0, KB), 1: slice(KB, 2 * KB)}.get(half if isinstance(half, int) else None, ALL)
        return blocks.at[some, pl.ds(pl.multiple_of(i * 16, 16), 16), :]

    def values_near():
        net.work(1.0, spread_values)
        ring_gather(net, NZ, z, "z", value_slice, 0.221, sparse_ready, VALUES)

    def gather(parts):
        counts = [[Count(2, lambda d=d, f=far: f(d)) for d in range(NX if x_first else NZ)] for x_first, _, _, far, _ in parts]

        def begin(half, way):
            far_way = {way: (ALL, 1.0), -way: (None, 0.0)}
            for (x_first, ref, size, _, urgency), count in zip(parts, counts):
                n, me, axis = (NX, x, "x") if x_first else (NZ, z, "z")
                ring(net, n, me, axis, lambda i, _, ref=ref: ref(i, half), size, lambda d, t=count: t[d](), far_way, urgency)
                count[0]()

        return (lambda: begin(yl, 1)), (lambda: begin(other, -1))

    def left_gather():
        parts = []
        for x_first, rows in ((True, slice(0, LEFT_A)), (False, slice(LEFT_A, 64))):
            everything = Count(NX if x_first else NZ, left_parts)
            size = (rows.stop - rows.start) * 0.131 / 128

            def near(i, h, x_first=x_first, rows=rows):
                return left.at[i, h, z, rows] if x_first else left.at[x, h, i, rows]

            def far(d, x_first=x_first, rows=rows, size=size, everything=everything):
                if x_first:
                    i = round_x(d)
                    ring_gather(net, NZ, z, "z", lambda k, h: left.at[i, h, k, rows], size, everything)
                else:
                    i = round_z(d)
                    ring_gather(net, NX, x, "x", lambda k, h: left.at[k, h, i, rows], size, everything)

            parts.append((x_first, near, size / 2, far, 0))
        return gather(parts)

    def right_gather():
        parts = []
        for p, (first, last) in enumerate(PARTS):
            x_first, span = p == 0, slice(first, last)
            everything = Count(NX if x_first else NZ, part_ready[p])
            size = (last - first) * 128e-6
            urgency = FAR if p < 2 else LATE

            def near(i, h, x_first=x_first, span=span):
                return right.at[i, h, z, :, :, span] if x_first else right.at[x, h, i, :, :, span]

            def far(d, x_first=x_first, span=span, size=size, everything=everything, urgency=urgency):
                if x_first:
                    i = round_x(d)
                    ring_gather(net, NZ, z, "z", lambda k, h: right.at[i, h, k, :, :, span], size, everything, urgency)
                else:
                    i = round_z(d)
                    ring_gather(net, NX, x, "x", lambda k, h: right.at[k, h, i, :, :, span], size, everything, urgency)

            parts.append((x_first, near, size / 2, far, NEAR if p < 2 else VALUES))
        return gather(parts)

    swap_left = net.copy(up_left, left.at[x, yl, z], pair)

    @pl.when(yl == 0)
    def _():
        swap_left.start()

    @pl.when(yl == 1)
    def _():
        net.copy(gate_left, left.at[x, yl, z], pair).start()

    at_first = (keeps[0], keeps[1], keeps[4])
    for made in at_first:
        made.wait()
    left_own, left_other = left_gather()
    right_own, right_other = right_gather()
    net.track(swap_left, "y", 0.033, left_other)
    swapped_right = Count(2, right_other)
    net.send(cols(gate_right, other), right.at[x, yl, z, 0], pair, "y", 0.057, swapped_right)
    net.send(cols(up_right, other), right.at[x, yl, z, 1], pair, "y", 0.057, swapped_right)
    net.send(
        shards.at[x, yl],
        shards.at[x, yl],
        pair,
        "y",
        0.033,
        lambda: ring_gather(net, NX, x, "x", lambda i, h: shards.at[i, h], 0.066, values_near, 1),
    )
    mine_half = pl.ds(pl.multiple_of(c * 64, 64), 64)
    sent_half = pl.ds(pl.multiple_of(yl * BLK + c * 64, 64), 64)
    got_half = pl.ds(pl.multiple_of(other * BLK + c * 64, 64), 64)
    net.send(
        tok.at[mine_half],
        t_all.at[sent_half],
        pair,
        "y",
        0.524,
        lambda: net.send(t_all.at[got_half], t_all.at[got_half], twin, "c", 0.524, tokens_there),
    )
    net.send(cols(grad_hidden, other), up_stream.at[own_rows], pair, "y", 0.459, lambda: None)
    left_own()
    right_own()
    for made in keeps[2:4]:
        made.wait()
    net.run()

    net.send(back, cols(hidden, yl), pair, "y", 0.459, lambda: None)

    def lot(i):
        return pl.ds(pl.multiple_of(i * 16, 16), 16)

    def to_owners(g):
        these = slice(g * KB, (g + 1) * KB)
        total = grads[these, lot(z), :] + came_up[3, these].astype(F32) + came_down[3, these].astype(F32)
        mine[g] = total.reshape(KB * 16, BLK)
        for s in range(8):
            for p in range(2):
                parcels[s, g, 0:KB, p * BLK : (p + 1) * BLK] = mine[g, pl.ds(p * 8 + s, KB, stride=16), :]
        for d in range(NX):
            for e in range(NL):
                if d == 0 and e == 0:
                    continue
                to_x, to_l = round_x(d), (yl if e == 0 else other)
                net.send(
                    parcels.at[to_x * 2 + to_l, g],
                    arrived_parcels.at[d * 2 + e, g],
                    {"x": to_x, "yl": to_l},
                    "owner",
                    0.033,
                    lambda: None,
                )

    def sum_round_z(g):
        begin, middle, end = g * KB, g * KB + 14, (g + 1) * KB
        home = Count(2, lambda: to_owners(g))

        def pass_on(way, j):
            came, leaves = (came_up, leave_up) if way == 1 else (came_down, leave_down)
            at = lot(round_z(way * (5 - j)))
            half, rest = (slice(begin, middle), slice(middle, end))[::way]
            these = half if j == 1 else slice(begin, end)
            if j == 1:
                leaves[0, half] = grads[half, at, :].astype(BF16)
            elif j == 2:
                leaves[1, half] = (grads[half, at, :] + came[0, half].astype(F32)).astype(BF16)
                leaves[1, rest] = grads[rest, at, :].astype(BF16)
            else:
                leaves[j - 1, these] = (grads[these, at, :] + came[j - 2, these].astype(F32)).astype(BF16)
            net.send(
                leaves.at[j - 1, these],
                came.at[j - 1, these],
                {"z": round_z(way)},
                "z+" if way == 1 else "z-",
                0.055 if j == 1 else 0.11,
                lambda: home() if j == 4 else pass_on(way, j + 1),
            )

        pass_on(1, 1)
        pass_on(-1, 1)

    for g, rows_ref, cols_ref in ((0, gate_rows, gate_cols), (1, up_rows, up_cols)):

        def gradient(i, _, g=g, rows_ref=rows_ref, cols_ref=cols_ref):
            for k in [i * 9 + u for u in range(9)]:
                col = cols_ref[k] - (yh * 2 + c) * 28 - yl * 14
                inside = (col >= 0) & (col < 14)
                term = dot(t_turn[rows_ref[k]], dpre[g * 14 + jnp.clip(col, 0, 13)])
                grads[g * KB + k] = jnp.where(inside, term, 0.0)
            return 0

        lax.fori_loop(0, KB // 9, gradient, 0)
        sum_round_z(g)
        net.now += 1.0
    net.run()
    total = parcels[x * 2 + yl]
    for i in range(1, 8):
        total = total + arrived_parcels[i]
    out_gate[...] = total[0, 0:KB]
    out_up[...] = total[1, 0:KB]
    net.finish()


def chains(gate_cols, up_cols, base):
    cols = jnp.stack([gate_cols, up_cols]) - base
    index = jnp.arange(64, dtype=jnp.int32)
    padded = jnp.pad(cols, ((0, 0), (0, 64 - KB)))
    asked = jnp.where(index < 32, padded, index - 32)
    limit = jnp.where(index < 32, index, KB)
    earlier = jnp.arange(KB, dtype=jnp.int32)
    hit = (cols[:, None, :] == asked[:, :, None]) & (earlier < limit[:, None])
    return jnp.max(jnp.where(hit, earlier + 1, 0), axis=2).reshape(128)


def on_device(*args):
    base = (lax.axis_index("yh") * 2 + lax.axis_index("c")) * 28
    table = chains(args[5], args[10], base)
    vmem, smem = pl.BlockSpec(memory_space=pltpu.VMEM), pl.BlockSpec(memory_space=pltpu.SMEM)
    hbm = pl.BlockSpec(memory_space=pl.ANY)
    specs = [hbm, hbm, hbm, vmem, smem, smem, hbm, hbm, vmem, smem, smem, hbm, smem]
    copies = 320
    return pl.pallas_call(
        kernel,
        out_shape=(
            jax.ShapeDtypeStruct((BLK, 2 * HALF), BF16),
            jax.ShapeDtypeStruct((KB, 2 * BLK), F32),
            jax.ShapeDtypeStruct((KB, 2 * BLK), F32),
        ),
        in_specs=specs,
        out_specs=(vmem, vmem, vmem),
        scratch_shapes=[
            pltpu.VMEM((2 * BLK, 4096), BF16),
            pltpu.VMEM((32, 2 * BLK, BLK), BF16),
            pltpu.VMEM((32, BLK, 2 * BLK), BF16),
            pltpu.VMEM((NX, NL, NZ, 64, TILE), BF16),
            pltpu.VMEM((NX, NL, NZ, 2, 16, HALF), BF16),
            pltpu.VMEM((NX, NL, 2, 32, 2 * BLK), BF16),
            pltpu.VMEM((2 * KB, BLK, BLK), BF16),
            pltpu.VMEM((8, 2 * BLK, TILE), BF16),
            pltpu.VMEM((2, 2 * BLK, TILE), F32),
            pltpu.VMEM((56, 2 * BLK, BLK), F32),
            pltpu.VMEM((2 * BLK, HALF), BF16),
            pltpu.VMEM((28, 2 * BLK, BLK), BF16),
            pltpu.VMEM((BLK, HALF), BF16),
            pltpu.VMEM((2 * KB, BLK, BLK), F32),
            pltpu.VMEM((4, 2 * KB, 16, BLK), BF16),
            pltpu.VMEM((4, 2 * KB, 16, BLK), BF16),
            pltpu.VMEM((4, 2 * KB, 16, BLK), BF16),
            pltpu.VMEM((4, 2 * KB, 16, BLK), BF16),
            pltpu.VMEM((2, KB * 16, BLK), F32),
            pltpu.VMEM((8, 2, 32, 2 * BLK), F32),
            pltpu.VMEM((8, 2, 32, 2 * BLK), F32),
            pltpu.SemaphoreType.DMA((copies,)),
            pltpu.SemaphoreType.DMA((copies,)),
            pltpu.SemaphoreType.DMA((8,)),
        ],
        compiler_params=pltpu.CompilerParams(
            collective_id=0, has_side_effects=True, vmem_limit_bytes=58 * 2**20
        ),
    )(*args, table)


def solution(mesh):
    finer = Mesh(mesh.devices.reshape(NX, NL, NZ, NH, NC), (*FSDP, *TP))
    return jax.shard_map(
        on_device,
        mesh=finer,
        in_specs=(
            P(FSDP, None),
            P(FSDP, TP),
            P(FSDP, TP),
            P(TP, FSDP),
            P(TP),
            P(TP),
            P(FSDP, TP),
            P(FSDP, TP),
            P(TP, FSDP),
            P(TP),
            P(TP),
            P(FSDP, TP),
        ),
        out_specs=(P(FSDP, TP), P(TP, FSDP), P(TP, FSDP)),
        check_vma=False,
    )
```
